32 devices in a mesh: groups: 2 (over y), img: 4 (over z), pair: 2 (over x), sub: 2 (over core).
Axes of the slice: x: 2, y: 2, z: 4, core: 2. Of those that a mesh axis runs over, the one named last changes fastest.
Arguments:
- descriptors: bfloat16 [16, 1024, 256], P(('groups', 'img', 'pair')), parts along dimension 0
- links: int32 [16, 3], P('groups'), parts along dimension 0, may hold values 0 or 1
- qk_weight: bfloat16 [256, 256], P(None, 'sub'), may hold values from -0.375 to 0.375
- value_weight: bfloat16 [256, 256], P(None, 'sub'), may hold values from -0.375 to 0.375
- out_weight: bfloat16 [256, 256], replicated, may hold values from -0.375 to 0.375
- mlp_in: bfloat16 [512, 512], replicated, may hold values from -0.25 to 0.25
- mlp_in_bias: float32 [512], replicated, may hold values from -4 to 4
- norm_gain: float32 [512], replicated, may hold values from 0.1 to 1.9
- norm_bias: float32 [512], replicated, may hold values from -3 to 3
- mlp_out: bfloat16 [512, 256], replicated, may hold values from -0.25 to 0.25
- mlp_out_bias: float32 [256], replicated, may hold values from -3 to 3
Outputs:
- updated: bfloat16 [16, 1024, 256], P(('groups', 'img', 'pair'), 'sub'), parts along dimension 0
The draws below stay inside these ranges and needn't reach their ends.
There are 2 independent parts, one for each index of `groups`. The reference program is written for one: setup_inputs(seed, part) draws one part's arguments, and reference() takes and returns one part's arrays. A program takes and returns all parts, laid end to end along the dimension named above; an argument that names none is the same for every part. Nothing has to cross between parts.
All inputs are finite; a program needn't handle non-finite values.
Results may differ from the reference program's by a relative error of at most 0.0045.
Values may be sent and summed in bfloat16 or wider, within the bound.
No kernel may reach another device: no remote copies, remote signals or barrier semaphores. Data moves between devices by JAX's collectives and lax.ppermute only.
A program may use at most 64 MiB of HBM per device.

```python
import math
import jax
import jax.numpy as jnp
from jax import lax

D = 256
HEADS = 4
HEAD = 64
KP = 1024
SPAN = 3
IMAGES = 8


def draw_descriptors(key, part):
    base_key, row_key, column_key = jax.random.split(key, 3)
    row_scale = jnp.exp(jax.random.uniform(row_key, (IMAGES, KP, 1), jnp.float32, 0.0, math.log(1.1)))
    column_scale = jnp.exp(jax.random.uniform(column_key, (1, 1, D), jnp.float32, -0.5 * math.log(3.0), 0.5 * math.log(3.0)))
    normal_part = jax.random.normal(base_key, (IMAGES, KP, D), jnp.float32) * 1.35
    values = normal_part * row_scale
    return (values * column_scale).astype(jnp.bfloat16)


def set_ends(values, rng, smallest, largest):
    shape = values.shape
    index_at = [jax.random.randint(jax.random.fold_in(rng, axis), (), 0, shape[axis]) for axis in range(len(shape))]
    values = values.at[tuple(index_at)].set(smallest)
    longest = shape.index(max(shape))
    index_at[longest] = (index_at[longest] + 1) % shape[longest]
    return values.at[tuple(index_at)].set(largest)


def shard_levels(stream_key, shape, cuts, smallest, top_value):
    loudness, own = 1.0, jax.random.fold_in(stream_key, 6)
    for dim, parts in cuts:
        heights = jnp.exp(jax.random.uniform(jax.random.fold_in(own, dim), (parts,), jnp.float32, smallest / len(cuts), top_value / len(cuts)))
        loudness = loudness * jnp.repeat(heights, shape[dim] // parts).reshape([-1 if axis == dim else 1 for axis in range(len(shape))])
    return loudness


def centred(stream_key, dims, scale, most, pieces=(), held_as=jnp.bfloat16):
    values = scale * jax.random.normal(stream_key, dims, jnp.float32)
    if pieces:
        values = values * shard_levels(stream_key, dims, pieces, -0.22, 0.18)
    return jnp.clip(values, -most, most).astype(held_as)


def setup_inputs(seed: int = 0, part: int = 0) -> dict:
    arg_keys = jax.random.split(jax.random.key(seed), 12)
    part_splits = jax.random.split(jax.random.fold_in(arg_keys[11], part), 12)
    descriptors = draw_descriptors(jax.random.fold_in(jax.random.fold_in(arg_keys[11], part), 71), part)
    links = set_ends((jax.random.randint(part_splits[1], (IMAGES, SPAN), 0, 4) < 3).astype(jnp.int32), jax.random.fold_in(part_splits[1], 1), 0, 1)
    qk_weight = centred(arg_keys[2], (D, D), D ** -0.5, 0.375, ((1, 2),))
    value_weight = centred(arg_keys[3], (D, D), D ** -0.5, 0.375, ((1, 2),))
    out_weight = centred(arg_keys[4], (D, D), D ** -0.5, 0.375)
    mlp_in = centred(arg_keys[5], (2 * D, 2 * D), (2 * D) ** -0.5, 0.25)
    mlp_in_bias = centred(arg_keys[6], (2 * D,), 1.0, 4.0, (), jnp.float32)
    norm_gain = jnp.clip(1.0 + 0.18 * jax.random.normal(arg_keys[7], (2 * D,), jnp.float32), 0.1, 1.9)
    norm_bias = centred(arg_keys[8], (2 * D,), 0.5, 3.0, (), jnp.float32)
    mlp_out = centred(arg_keys[9], (2 * D, D), (2 * D) ** -0.5, 0.25)
    mlp_out_bias = centred(arg_keys[10], (D,), 0.5, 3.0, (), jnp.float32)
    return {"descriptors": descriptors, "links": links, "qk_weight": qk_weight, "value_weight": value_weight, "out_weight": out_weight, "mlp_in": mlp_in, "mlp_in_bias": mlp_in_bias, "norm_gain": norm_gain, "norm_bias": norm_bias, "mlp_out": mlp_out, "mlp_out_bias": mlp_out_bias}


def held(array_value):
    return lax.optimization_barrier(array_value).astype(jnp.float32)

def pair_terms(keys_lower, values_lower, keys_upper, values_upper):
    score_scale = 1.0 / math.sqrt(HEAD)
    query_part = held(keys_lower).reshape(KP, HEADS, HEAD)
    key_part = held(keys_upper).reshape(KP, HEADS, HEAD)
    scores = jnp.einsum('qhd,khd->hqk', query_part, key_part) * score_scale
    row_weights = jax.nn.softmax(scores, axis=2).astype(jnp.bfloat16)
    column_weights = jax.nn.softmax(scores, axis=1).astype(jnp.bfloat16)
    value_upper = held(values_upper).reshape(KP, HEADS, HEAD)
    value_lower = held(values_lower).reshape(KP, HEADS, HEAD)
    to_lower = jnp.einsum('hqk,khd->qhd', held(row_weights), value_upper)
    to_upper = jnp.einsum('hqk,qhd->khd', held(column_weights), value_lower)
    return (to_lower.reshape(KP, D).astype(jnp.bfloat16), to_upper.reshape(KP, D).astype(jnp.bfloat16))

def reference(descriptors, links, qk_weight, value_weight, out_weight, mlp_in, mlp_in_bias, norm_gain, norm_bias, mlp_out, mlp_out_bias):
    flat_rows = descriptors.reshape(IMAGES * KP, D)
    key_rows = jnp.dot(flat_rows, qk_weight, preferred_element_type=jnp.float32).astype(jnp.bfloat16).reshape(IMAGES, KP, D)
    value_rows = jnp.dot(flat_rows, value_weight, preferred_element_type=jnp.float32).astype(jnp.bfloat16).reshape(IMAGES, KP, D)
    summed = jnp.zeros((IMAGES, KP, D), jnp.float32)
    for step_size in range(1, SPAN + 1):
        pair_count = IMAGES - step_size

        def one_pair(lower_image):
            upper_image = lower_image + step_size
            return pair_terms(key_rows[lower_image], value_rows[lower_image], key_rows[upper_image], value_rows[upper_image])
        to_lower, to_upper = lax.map(one_pair, jnp.arange(pair_count, dtype=jnp.int32))
        linked = links[:pair_count, step_size - 1].astype(jnp.float32)[:, None, None]
        summed = summed.at[:pair_count].add(linked * to_lower.astype(jnp.float32))
        summed = summed.at[step_size:].add(linked * to_upper.astype(jnp.float32))
    summed_b = summed.astype(jnp.bfloat16).reshape(IMAGES * KP, D)
    projected = jnp.dot(summed_b, out_weight, preferred_element_type=jnp.float32).astype(jnp.bfloat16)
    hidden = jnp.dot(flat_rows, mlp_in[:D], preferred_element_type=jnp.float32)
    hidden = hidden + jnp.dot(projected, mlp_in[D:], preferred_element_type=jnp.float32) + mlp_in_bias
    mean_value = lax.optimization_barrier(jnp.mean(hidden, axis=1, keepdims=True))
    centered = hidden - mean_value
    variance = lax.optimization_barrier(jnp.mean(centered * centered, axis=1, keepdims=True))
    normed = centered * lax.rsqrt(variance + 1e-05) * norm_gain + norm_bias
    activated = jax.nn.gelu(normed, approximate=False).astype(jnp.bfloat16)
    output_rows = jnp.dot(activated, mlp_out, preferred_element_type=jnp.float32) + mlp_out_bias
    output_rows = output_rows + flat_rows.astype(jnp.float32)
    return output_rows.astype(jnp.bfloat16).reshape(IMAGES, KP, D)
```

```python
import functools
import math

import jax
import jax.numpy as jnp
from jax import lax
from jax.experimental import pallas as pl
from jax.experimental.pallas import tpu as pltpu
from jax.sharding import PartitionSpec as P

HEADS = 4
SPAN = 3
RING = ("img", "pair", "sub")
SCORE_LIMIT = 75.0
VALUE_LIMIT = 256.0
F32 = jnp.float32
BF16 = jnp.bfloat16
VMEM = pl.BlockSpec(memory_space=pltpu.VMEM)
SMEM = pl.BlockSpec(memory_space=pltpu.SMEM)


def dot(a, b, contract=(1, 0)):
    return lax.dot_general(
        a, b, (((contract[0],), (contract[1],)), ((), ())), preferred_element_type=F32
    )


def largest_norms(keys, head_width):
    squares = keys.astype(F32)
    squares = (squares * squares * 1.01).astype(BF16)
    width = keys.shape[1]
    head_of = lax.broadcasted_iota(jnp.int32, (width, 128), 0) // head_width
    lane = lax.broadcasted_iota(jnp.int32, (width, 128), 1)
    sums = dot(squares, jnp.where(head_of == lane, 1.0, 0.0).astype(BF16))
    return jnp.max(sums, axis=0, keepdims=True)


def prologue_kernel(
    place_ref, x_ref, own_ref, other_ref, mlp_ref, bias_ref, wkv_ref, keys_ref, norm_ref, hidden_ref
):
    rows, width = x_ref.shape
    local = width // 2
    sub = lax.rem(place_ref[0], 2)
    for part in range(2):
        own = own_ref[:, part * local : (part + 1) * local]
        other = other_ref[:, part * local : (part + 1) * local]
        start = part * width
        wkv_ref[:, start : start + local] = jnp.where(sub == 0, own, other)
        wkv_ref[:, start + local : start + width] = jnp.where(sub == 0, other, own)
    keys = dot(x_ref[...], wkv_ref[:, :width]).astype(BF16)
    keys_ref[...] = keys
    norm_ref[...] = jnp.broadcast_to(largest_norms(keys, width // HEADS), norm_ref.shape)
    half = rows // 2
    own_rows = x_ref[pl.ds(pl.multiple_of(sub * half, half), half), :]
    hidden_ref[...] = dot(own_rows, mlp_ref[:width, :]) + bias_ref[...]


def partner_kernel(
    step, images, last, place_ref, links_ref, keys_ref, norm_ref, x_ref, wkv_ref, *refs
):
    if last:
        first_ref, second_ref, keep_ref, send_ref, message_ref, kh_ref, vh_ref = refs
    else:
        message_ref, kh_ref, vh_ref = refs
    rows, width = keys_ref.shape
    head_width = width // HEADS
    scale = 1.0 / math.sqrt(head_width)
    image = place_ref[0] // 2
    sub = lax.rem(place_ref[0], 2)
    lower = image - sub * step
    inside = jnp.logical_and(lower >= 0, lower + step < images)
    entry = links_ref[step - 1, jnp.clip(lower, 0, images - 1)]
    linked = jnp.logical_and(inside, entry != 0)
    tile = 256
    lane = lax.broadcasted_iota(jnp.int32, (tile, 128), 1)

    @pl.when(jnp.logical_not(linked))
    def _():
        message_ref[...] = jnp.zeros_like(message_ref)

    @pl.when(linked)
    def _():
        norms = jnp.zeros((1, 128), F32)
        largest = jnp.zeros((tile, width), F32)
        for r in range(0, rows, tile):
            both = dot(x_ref[r : r + tile, :], wkv_ref[...]).astype(BF16)
            keys, values = both[:, :width], both[:, width:]
            norms = jnp.maximum(norms, largest_norms(keys, head_width))
            largest = jnp.maximum(largest, jnp.abs(values.astype(F32)))
            for head in range(HEADS):
                block, odd = head // 2 * 128, head % 2
                mine = (lane >= 64) if odd else (lane < 64)
                ones = jnp.where(lane == (0 if odd else 64), 1.0, 0.0).astype(BF16)
                kh_ref[head, r : r + tile, :] = jnp.where(
                    mine, keys[:, block : block + 128], jnp.zeros((), BF16)
                )
                vh_ref[head, r : r + tile, :] = jnp.where(
                    mine, values[:, block : block + 128], ones
                )
        bound = jnp.max(norms * norm_ref[0:1, :]) * (scale * scale)
        safe = jnp.logical_and(
            bound <= SCORE_LIMIT * SCORE_LIMIT, jnp.max(largest) <= VALUE_LIMIT
        )

        def heads_of(r, weights):
            for block in range(HEADS // 2):
                queries = keys_ref[pl.ds(r, tile), block * 128 : (block + 1) * 128]
                parts = []
                for odd in range(2):
                    head = 2 * block + odd
                    scores = dot(queries, kh_ref[head], (1, 1))
                    product = dot(weights(scores), vh_ref[head])
                    at = 0 if odd else 64
                    parts.append(product / product[:, at : at + 1])
                message_ref[pl.ds(r, tile), block * 128 : (block + 1) * 128] = jnp.where(
                    lane < 64, parts[0], parts[1]
                ).astype(BF16)

        @pl.when(safe)
        def _():
            def body(i, carry):
                heads_of(
                    pl.multiple_of(i * tile, tile),
                    lambda s: jnp.exp2(s * (scale * math.log2(math.e))).astype(BF16),
                )
                return carry

            lax.fori_loop(0, rows // tile, body, 0)

        @pl.when(jnp.logical_not(safe))
        def _():
            def weights(s):
                s = s * scale
                e = jnp.exp(s - jnp.max(s, axis=1, keepdims=True))
                return (e / jnp.sum(e, axis=1, keepdims=True)).astype(BF16)

            def body(i, carry):
                heads_of(pl.multiple_of(i * tile, tile), weights)
                return carry

            lax.fori_loop(0, rows // tile, body, 0)

    if last:
        half = rows // 2
        for out_ref, which in ((keep_ref, sub), (send_ref, 1 - sub)):
            at = pl.ds(pl.multiple_of(which * half, half), half)
            total = first_ref[at, :].astype(F32) + second_ref[at, :].astype(F32)
            total = total + message_ref[at, :].astype(F32)
            out_ref[...] = total.astype(out_ref.dtype)


def tail_kernel(
    place_ref, keep_ref, came_ref, hidden_ref, x_ref, out_ref, mlp_ref, gain_ref, shift_ref,
    mlp_out_ref, out_bias_ref, result_ref,
):
    rows, width = keep_ref.shape
    sub = lax.rem(place_ref[0], 2)
    summed = (keep_ref[...] + came_ref[...].astype(F32)).astype(BF16)
    projected = dot(summed, out_ref[...]).astype(BF16)
    hidden = hidden_ref[...] + dot(projected, mlp_ref[width:, :])
    centered = hidden - jnp.mean(hidden, axis=1, keepdims=True)
    variance = jnp.mean(centered * centered, axis=1, keepdims=True)
    normed = centered * lax.rsqrt(variance + 1e-05) * gain_ref[...] + shift_ref[...]
    activated = (0.5 * normed * (1.0 + lax.erf(normed * math.sqrt(0.5)))).astype(BF16)
    own_rows = x_ref[pl.ds(pl.multiple_of(sub * rows, rows), rows), :].astype(F32)
    updated = dot(activated, mlp_out_ref[...]) + out_bias_ref[...]
    result_ref[...] = (updated + own_rows).astype(BF16)


def shape(dims, dtype):
    return jax.ShapeDtypeStruct(dims, dtype)


def cost(flops, moved, exps=0):
    return pl.CostEstimate(flops=flops, bytes_accessed=moved, transcendentals=exps)


def on_device(
    descriptors,
    links,
    qk_weight,
    value_weight,
    out_weight,
    mlp_in,
    mlp_in_bias,
    norm_gain,
    norm_bias,
    mlp_out,
    mlp_out_bias,
):
    own = descriptors[0]
    rows, width = own.shape
    hidden_width = mlp_in.shape[1]
    images = lax.axis_size(("img", "pair"))
    place = lax.axis_index(RING).reshape(1)
    links_t = links.T
    params = pltpu.CompilerParams(vmem_limit_bytes=40 << 20)

    own_weights = jnp.concatenate([qk_weight, value_weight], axis=1)
    other_weights = lax.ppermute(own_weights, "sub", [(0, 1), (1, 0)])

    def fetched(step):
        pairs = []
        for image in range(images):
            if image - step >= 0:
                pairs.append((2 * image, 2 * (image - step)))
            if image + step < images:
                pairs.append((2 * image + 1, 2 * (image + step) + 1))
        return lax.ppermute(own, RING, pairs)

    steps = [2, 1, 3]
    partners = [fetched(step) for step in steps]

    wkv, keys, norms, hidden = pl.pallas_call(
        prologue_kernel,
        in_specs=[SMEM] + [VMEM] * 5,
        out_specs=[VMEM] * 4,
        out_shape=[
            shape((width, 2 * width), BF16),
            shape((rows, width), BF16),
            shape((8, 128), F32),
            shape((rows // 2, hidden_width), F32),
        ],
        compiler_params=params,
        cost_estimate=cost(4 * rows * width * width, 4 << 20),
        name="prologue",
    )(place, own, own_weights, other_weights, mlp_in, mlp_in_bias.reshape(1, -1))

    messages = []
    for step, partner in zip(steps, partners):
        last = step == steps[-1]
        out_shape = [shape((rows, width), BF16)]
        if last:
            out_shape = [shape((rows // 2, width), F32), shape((rows // 2, width), BF16)]
        scratch = [pltpu.VMEM((HEADS, rows, 128), BF16)] * 2
        if last:
            scratch = [pltpu.VMEM((rows, width), BF16)] + scratch
        got = pl.pallas_call(
            functools.partial(partner_kernel, step, images, last),
            in_specs=[SMEM, SMEM] + [VMEM] * (6 if last else 4),
            out_specs=[VMEM] * len(out_shape),
            out_shape=out_shape,
            scratch_shapes=scratch,
            compiler_params=params,
            cost_estimate=cost(8 * rows * rows * width, 2 << 20, HEADS * rows * rows),
            name=f"partner_{step}",
        )(place, links_t, keys, norms, partner, wkv, *(messages if last else ()))
        messages.extend(got)
    keep, send = messages[-2:]
    came = lax.ppermute(send, "sub", [(0, 1), (1, 0)])

    result = pl.pallas_call(
        tail_kernel,
        in_specs=[SMEM] + [VMEM] * 10,
        out_specs=VMEM,
        out_shape=shape((rows // 2, width), BF16),
        compiler_params=params,
        cost_estimate=cost(4 * rows * width * width, 4 << 20),
        name="tail",
    )(
        place, keep, came, hidden, own, out_weight, mlp_in, norm_gain.reshape(1, -1),
        norm_bias.reshape(1, -1), mlp_out, mlp_out_bias.reshape(1, -1),
    )
    return result[None]


def solution(mesh):
    placed = (
        P(("groups", "img", "pair"), None, None),
        P("groups", None),
        P(None, "sub"),
        P(None, "sub"),
        P(),
        P(),
        P(),
        P(),
        P(),
        P(),
        P(),
    )
    return jax.shard_map(
        on_device,
        mesh=mesh,
        in_specs=placed,
        out_specs=P(("groups", "img", "pair"), "sub", None),
        check_vma=False,
    )
```

```python
import functools
import math

import jax
import jax.numpy as jnp
from jax import lax
from jax.experimental import pallas as pl
from jax.experimental.pallas import tpu as pltpu
from jax.sharding import PartitionSpec as P

HEADS = 4
SPAN = 3
RING = ("img", "pair", "sub")
SCORE_LIMIT = 75.0
VALUE_LIMIT = 256.0
F32 = jnp.float32
BF16 = jnp.bfloat16
VMEM = pl.BlockSpec(memory_space=pltpu.VMEM)
SMEM = pl.BlockSpec(memory_space=pltpu.SMEM)
HBM = pl.BlockSpec(memory_space=pltpu.HBM)


def dot(a, b, contract=(1, 0)):
    return lax.dot_general(
        a, b, (((contract[0],), (contract[1],)), ((), ())), preferred_element_type=F32
    )


def largest_norms(keys, head_width):
    squares = keys.astype(F32)
    squares = (squares * squares * 1.01).astype(BF16)
    width = keys.shape[1]
    head_of = lax.broadcasted_iota(jnp.int32, (width, 128), 0) // head_width
    lane = lax.broadcasted_iota(jnp.int32, (width, 128), 1)
    sums = dot(squares, jnp.where(head_of == lane, 1.0, 0.0).astype(BF16))
    return jnp.max(sums, axis=0, keepdims=True)


def prologue_kernel(
    images, place_ref, links_ref, x_hbm, qk_hbm, value_hbm, qk_other_ref, value_other_ref, mlp_hbm,
    bias_hbm, gain_hbm, shift_hbm, out_bias_hbm, wk_ref, wvt_ref, queries_ref, facts_ref,
    hidden_ref, rows_ref, vectors_ref, x_ref, qk_ref, value_ref, mlp_ref, bias_ref, small_ref, out_bias_ref, sems,
):
    rows, width = x_ref.shape
    head_width = width // HEADS
    local = width // 2
    sub = lax.rem(place_ref[0], 2)
    image = place_ref[0] // 2
    copies = [
        pltpu.make_async_copy(source, target, sems.at[i])
        for i, (source, target) in enumerate(
            [
                (qk_hbm, qk_ref),
                (value_hbm, value_ref),
                (x_hbm, x_ref),
                (mlp_hbm.at[0:width], mlp_ref),
                (bias_hbm, bias_ref),
                (gain_hbm, small_ref.at[0:1]),
                (shift_hbm, small_ref.at[1:2]),
                (out_bias_hbm, out_bias_ref),
            ]
        )
    ]
    for copy in copies:
        copy.start()
    copies[0].wait()
    copies[1].wait()
    values = []
    for own_ref, other_ref in ((qk_ref, qk_other_ref), (value_ref, value_other_ref)):
        own, other = own_ref[...], other_ref[...]
        values.append(jnp.where(sub == 0, own, other))
        values.append(jnp.where(sub == 0, other, own))
    wk_ref[:, :local], wk_ref[:, local:] = values[0], values[1]
    wvt_ref[:local, :], wvt_ref[local:, :] = values[2].T, values[3].T
    for copy in copies[2:]:
        copy.wait()
    keys = dot(x_ref[...], wk_ref[...]).astype(BF16)
    lane = lax.broadcasted_iota(jnp.int32, (rows, 128), 1)
    for head in range(HEADS):
        block, odd = head // 2 * 128, head % 2
        mine = (lane >= 64) if odd else (lane < 64)
        queries_ref[head] = jnp.where(mine, keys[:, block : block + 128], jnp.zeros((), BF16))
    facts_ref[0:1, :] = largest_norms(keys, head_width)
    for step in range(1, SPAN + 1):
        lower = image - sub * step
        inside = jnp.logical_and(lower >= 0, lower + step < images)
        entry = links_ref[step - 1, jnp.clip(lower, 0, images - 1)]
        linked = jnp.where(jnp.logical_and(inside, entry != 0), 1.0, 0.0)
        facts_ref[step : step + 1, :] = jnp.full((1, 128), linked, F32)
    half = rows // 2
    own_rows = x_ref[pl.ds(pl.multiple_of(sub * half, half), half), :]
    rows_ref[...] = own_rows
    hidden_ref[...] = dot(own_rows, mlp_ref[...]) + bias_ref[...]
    vectors_ref[0:2, :] = small_ref[0:2, :]
    vectors_ref[2:3, :width] = out_bias_ref[...]


def partner_kernel(step, two, last, place_ref, queries_ref, facts_ref, x_ref, *refs):
    if two:
        other_ref, *refs = refs
    wk_ref, wvt_ref, *refs = refs
    if last:
        first_ref, second_ref, keep_ref, send_ref, message_ref, keys_ref, values_ref = refs
    else:
        message_ref, keys_ref, values_ref = refs
    rows, width = keys_ref.shape
    head_width = width // HEADS
    scale = 1.0 / math.sqrt(head_width)
    place = place_ref[0]
    sub = lax.rem(place, 2)
    linked = jnp.max(facts_ref[step : step + 1, :]) > 0.0
    tile = 256

    @pl.when(jnp.logical_not(linked))
    def _():
        message_ref[...] = jnp.zeros_like(message_ref)

    @pl.when(linked)
    def _():
        norms = jnp.zeros((1, 128), F32)
        largest = jnp.zeros((width, tile), F32)
        for r in range(0, rows, tile):
            x = x_ref[r : r + tile, :]
            if two:
                x = jnp.where(lax.rem(place // 2, 2) == sub, other_ref[r : r + tile, :], x)
            keys = dot(x, wk_ref[...]).astype(BF16)
            keys_ref[r : r + tile, :] = keys
            norms = jnp.maximum(norms, largest_norms(keys, head_width))
            values = dot(wvt_ref[...], x, (1, 1)).astype(BF16)
            largest = jnp.maximum(largest, jnp.abs(values.astype(F32)))
            for head in range(HEADS):
                values_ref[head, :head_width, r : r + tile] = values[
                    head * head_width : (head + 1) * head_width, :
                ]
                values_ref[head, head_width:, r : r + tile] = jnp.ones((16, tile), BF16)
        bound = jnp.max(norms * facts_ref[0:1, :]) * (scale * scale)
        safe = jnp.logical_and(
            bound <= SCORE_LIMIT * SCORE_LIMIT, jnp.max(largest) <= VALUE_LIMIT
        )

        @pl.when(safe)
        def _():
            wide = rows // 2

            def body(i, carry):
                at = pl.ds(pl.multiple_of(i * wide, wide), wide)
                totals = {}

                def finish(head, r, scores):
                    weights = jnp.exp2(scores * (scale * math.log2(math.e))).astype(BF16)
                    product = dot(values_ref[head, :, r : r + tile], weights)
                    total = product if r == 0 else totals[head] + product
                    totals[head] = total
                    if r + tile == rows:
                        inverse = 1.0 / total[head_width : head_width + 1]
                        message_ref[head * head_width : (head + 1) * head_width, at] = (
                            total[:head_width] * inverse
                        ).astype(BF16)

                waiting = None
                for head in range(HEADS):
                    queries = queries_ref[head, at, :]
                    lanes = slice(head // 2 * 128, head // 2 * 128 + 128)
                    for r in range(0, rows, tile):
                        scores = dot(keys_ref[r : r + tile, lanes], queries, (1, 1))
                        if waiting is not None:
                            finish(*waiting)
                        waiting = (head, r, scores)
                finish(*waiting)
                return carry

            lax.fori_loop(0, rows // wide, body, 0)

        @pl.when(jnp.logical_not(safe))
        def _():
            def body(i, carry):
                head, at = i // (rows // tile), lax.rem(i, rows // tile)
                at = pl.ds(pl.multiple_of(at * tile, tile), tile)
                lanes = pl.ds(pl.multiple_of(head // 2 * 128, 128), 128)
                scores = dot(keys_ref[:, lanes], queries_ref[head, at, :], (1, 1)) * scale
                powers = jnp.exp(scores - jnp.max(scores, axis=0, keepdims=True))
                weights = powers / jnp.sum(powers, axis=0, keepdims=True)
                product = dot(values_ref[head, :head_width, :], weights.astype(BF16))
                into = pl.ds(pl.multiple_of(head * head_width, head_width), head_width)
                message_ref[into, at] = product.astype(BF16)
                return carry

            lax.fori_loop(0, HEADS * (rows // tile), body, 0)

    if last:
        half = rows // 2
        for out_ref, which in ((keep_ref, sub), (send_ref, 1 - sub)):
            at = pl.ds(pl.multiple_of(which * half, half), half)
            total = first_ref[:, at].astype(F32) + second_ref[:, at].astype(F32)
            total = total + message_ref[:, at].astype(F32)
            out_ref[...] = total.astype(out_ref.dtype)


def tail_kernel(
    keep_ref, came_ref, hidden_ref, rows_ref, out_ref, mlp_ref, vectors_ref, mlp_out_ref, result_ref
):
    width = keep_ref.shape[0]
    summed = (keep_ref[...] + came_ref[...].astype(F32)).astype(BF16)
    projected = dot(summed, out_ref[...], (0, 0)).astype(BF16)
    hidden = hidden_ref[...] + dot(projected, mlp_ref[width:, :])
    centered = hidden - jnp.mean(hidden, axis=1, keepdims=True)
    variance = jnp.mean(centered * centered, axis=1, keepdims=True)
    normed = centered * lax.rsqrt(variance + 1e-05) * vectors_ref[0:1, :] + vectors_ref[1:2, :]
    activated = (0.5 * normed * (1.0 + lax.erf(normed * math.sqrt(0.5)))).astype(BF16)
    updated = dot(activated, mlp_out_ref[...]) + vectors_ref[2:3, :width]
    result_ref[...] = (updated + rows_ref[...].astype(F32)).astype(BF16)


def shape(dims, dtype):
    return jax.ShapeDtypeStruct(dims, dtype)


def cost(flops, moved, exps=0):
    return pl.CostEstimate(flops=flops, bytes_accessed=moved, transcendentals=exps)


def on_device(
    descriptors,
    links,
    qk_weight,
    value_weight,
    out_weight,
    mlp_in,
    mlp_in_bias,
    norm_gain,
    norm_bias,
    mlp_out,
    mlp_out_bias,
):
    own = descriptors[0]
    rows, width = own.shape
    hidden_width = mlp_in.shape[1]
    half = rows // 2
    images = lax.axis_size(("img", "pair"))
    place = lax.axis_index(RING).reshape(1)
    params = pltpu.CompilerParams(vmem_limit_bytes=40 << 20)

    swap = [(0, 1), (1, 0)]
    qk_other = lax.ppermute(qk_weight, "sub", swap)
    value_other = lax.ppermute(value_weight, "sub", swap)

    def carried(value, moves):
        pairs = []
        for image in range(images):
            for sub in range(2):
                source = moves(image, sub)
                if source is not None:
                    pairs.append((2 * source[0] + source[1], 2 * image + sub))
        return lax.ppermute(value, RING, pairs)

    def ahead(image, sub, step):
        partner = image + step if sub == 0 else image - step
        return partner if 0 <= partner < images else None

    def by_two(image, sub):
        partner = ahead(image, sub, 2)
        return None if partner is None else (partner, sub)

    def within(image, sub):
        return (image ^ 1, image % 2) if image % 2 == sub else None

    def across(image, sub):
        partner = ahead(image, sub, 1)
        return None if image % 2 == sub or partner is None else (image ^ 1, sub)

    def onward(image, sub):
        return None if ahead(image, sub, 3) is None else (ahead(image, sub, 2), sub)

    def onward_inner(image, sub):
        return onward(image, sub) if image % 2 == sub else None

    def onward_outer(image, sub):
        return None if image % 2 == sub else onward(image, sub)

    two = carried(own, by_two)
    inner = carried(own, within)

    wk, wvt, queries, facts, hidden, own_half, vectors = pl.pallas_call(
        functools.partial(prologue_kernel, images),
        in_specs=[SMEM, SMEM] + [HBM] * 3 + [VMEM] * 2 + [HBM] * 5,
        out_specs=[VMEM] * 7,
        out_shape=[
            shape((width, width), BF16),
            shape((width, width), BF16),
            shape((HEADS, rows, 128), BF16),
            shape((8, 128), F32),
            shape((half, hidden_width), F32),
            shape((half, width), BF16),
            shape((8, hidden_width), F32),
        ],
        scratch_shapes=[
            pltpu.VMEM((rows, width), BF16),
            pltpu.VMEM(qk_weight.shape, BF16),
            pltpu.VMEM(qk_weight.shape, BF16),
            pltpu.VMEM((width, hidden_width), BF16),
            pltpu.VMEM((1, hidden_width), F32),
            pltpu.VMEM((8, hidden_width), F32),
            pltpu.VMEM((1, width), F32),
            pltpu.SemaphoreType.DMA((8,)),
        ],
        compiler_params=params,
        cost_estimate=cost(4 * rows * width * width, 4 << 20),
        name="prologue",
    )(
        place, links.T, own, qk_weight, value_weight, qk_other, value_other, mlp_in,
        mlp_in_bias.reshape(1, -1), norm_gain.reshape(1, -1), norm_bias.reshape(1, -1),
        mlp_out_bias.reshape(1, -1),
    )

    def attended(step, partner, before):
        last = step == SPAN
        out_shape = [shape((width, rows), BF16)]
        scratch = [pltpu.VMEM((rows, width), BF16)]
        scratch += [pltpu.VMEM((HEADS, width // HEADS + 16, rows), BF16)]
        if last:
            out_shape = [shape((width, half), F32), shape((width, half), BF16)]
            scratch = [pltpu.VMEM((width, rows), BF16)] + scratch
        args = [place, queries, facts, *partner, wk, wvt, *before]
        return pl.pallas_call(
            functools.partial(partner_kernel, step, len(partner) == 2, last),
            in_specs=[SMEM] + [VMEM] * (len(args) - 1),
            out_specs=[VMEM] * len(out_shape),
            out_shape=out_shape,
            scratch_shapes=scratch,
            compiler_params=params,
            cost_estimate=cost(8 * rows * rows * width, 2 << 20, HEADS * rows * rows),
            name=f"partner_{step}",
        )(*args)

    two, inner, facts = lax.optimization_barrier((two, inner, facts))
    outer = carried(two, across)
    inner_far = carried(inner, onward_inner)
    (message_two,) = attended(2, [two], [])
    outer, message_two = lax.optimization_barrier((outer, message_two))
    outer_far = carried(outer, onward_outer)
    (message_one,) = attended(1, [outer, inner], [])
    inner_far, outer_far, message_one = lax.optimization_barrier(
        (inner_far, outer_far, message_one)
    )
    keep, send = attended(3, [outer_far, inner_far], [message_two, message_one])
    came = lax.ppermute(send, "sub", swap)

    result = pl.pallas_call(
        tail_kernel,
        in_specs=[VMEM] * 8,
        out_specs=VMEM,
        out_shape=shape((half, width), BF16),
        compiler_params=params,
        cost_estimate=cost(4 * rows * width * width, 4 << 20),
        name="tail",
    )(keep, came, hidden, own_half, out_weight, mlp_in, vectors, mlp_out)
    return result[None]


def solution(mesh):
    placed = (
        P(("groups", "img", "pair"), None, None),
        P("groups", None),
        P(None, "sub"),
        P(None, "sub"),
        P(),
        P(),
        P(),
        P(),
        P(),
        P(),
        P(),
    )
    return jax.shard_map(
        on_device,
        mesh=mesh,
        in_specs=placed,
        out_specs=P(("groups", "img", "pair"), "sub", None),
        check_vma=False,
    )
```

```python
import functools
import math

import jax
import jax.numpy as jnp
from jax import lax
from jax.experimental import pallas as pl
from jax.experimental.pallas import tpu as pltpu
from jax.sharding import PartitionSpec as P


HEADS = 4
SPAN = 3
RING = ("img", "pair", "sub")
LEAST_SUM, LARGEST_SUM = 1e-20, 1e20
LARGEST_PRODUCT = 1e37
F32 = jnp.float32
BF16 = jnp.bfloat16
VMEM = pl.BlockSpec(memory_space=pltpu.VMEM)
SMEM = pl.BlockSpec(memory_space=pltpu.SMEM)


def dot(a, b, contract=(1, 0)):
    return lax.dot_general(
        a, b, (((contract[0],), (contract[1],)), ((), ())), preferred_element_type=F32
    )


def prologue_kernel(
    images, place_ref, links_ref, x_ref, qk_ref, value_ref, qk_other_ref, value_other_ref, gain_ref,
    shift_ref, bias_ref, out_bias_ref, wk_ref, wvt_ref, queries_ref, facts_ref, vectors_ref,
):
    rows, width = x_ref.shape
    local = width // 2
    sub = lax.rem(place_ref[0], 2)
    image = place_ref[0] // 2
    parts = []
    for own_ref, other_ref in ((qk_ref, qk_other_ref), (value_ref, value_other_ref)):
        own, other = own_ref[...], other_ref[...]
        parts.append(jnp.where(sub == 0, own, other))
        parts.append(jnp.where(sub == 0, other, own))
    wk_ref[:, :local], wk_ref[:, local:] = parts[0], parts[1]
    wvt_ref[:local, :], wvt_ref[local:, :] = parts[2].T, parts[3].T
    keys = dot(x_ref[...], wk_ref[...]).astype(BF16)
    lane = lax.broadcasted_iota(jnp.int32, (rows, 128), 1)
    for head in range(HEADS):
        block, odd = head // 2 * 128, head % 2
        mine = (lane >= 64) if odd else (lane < 64)
        queries_ref[head] = jnp.where(mine, keys[:, block : block + 128], jnp.zeros((), BF16))
    for step in range(1, SPAN + 1):
        lower = image - sub * step
        inside = jnp.logical_and(lower >= 0, lower + step < images)
        entry = links_ref[step - 1, jnp.clip(lower, 0, images - 1)]
        linked = jnp.where(jnp.logical_and(inside, entry != 0), 1.0, 0.0)
        facts_ref[step : step + 1, :] = jnp.full((1, 128), linked, F32)
    vectors_ref[0:1, :] = gain_ref[...]
    vectors_ref[1:2, :] = shift_ref[...]
    vectors_ref[2:3, :] = bias_ref[...]
    vectors_ref[3:4, :width] = out_bias_ref[...]


def project(x_ref, other_ref, take_other, wk_ref, wvt_ref, keys_ref, values_ref):
    rows, width = keys_ref.shape
    head_width = width // HEADS
    tile = 256
    for r in range(0, rows, tile):
        x = x_ref[r : r + tile, :]
        if other_ref is not None:
            x = jnp.where(take_other, other_ref[r : r + tile, :], x)
        keys_ref[r : r + tile, :] = dot(x, wk_ref[...]).astype(BF16)
        values = dot(wvt_ref[...], x, (1, 1)).astype(BF16)
        for head in range(HEADS):
            values_ref[head, :head_width, r : r + tile] = values[
                head * head_width : (head + 1) * head_width, :
            ]
            values_ref[head, head_width:, r : r + tile] = jnp.ones((16, tile), BF16)


def attend(queries_ref, at, span, keys_ref, values_ref, message_ref, into):
    rows, width = keys_ref.shape
    head_width = width // HEADS
    scale = 1.0 / math.sqrt(head_width)
    tile = 256
    queries_at = pl.ds(pl.multiple_of(at, span), span)
    totals = {}
    wrong = []

    def finish(head, r, scores):
        weights = jnp.exp2(scores * (scale * math.log2(math.e))).astype(BF16)
        product = dot(values_ref[head, :, r : r + tile], weights)
        total = product if r == 0 else totals[head] + product
        totals[head] = total
        if r + tile == rows:
            sums = total[head_width : head_width + 1]
            message_ref[head * head_width : (head + 1) * head_width, into] = (
                total[:head_width] * (1.0 / sums)
            ).astype(BF16)
            top = jnp.max(jnp.abs(total[:head_width]), axis=0, keepdims=True)
            fine = jnp.logical_and(sums > LEAST_SUM, sums < LARGEST_SUM)
            fine = jnp.logical_and(fine, top < LARGEST_PRODUCT)
            wrong.append(jnp.where(fine, 0.0, 1.0))

    waiting = []
    for head in range(HEADS):
        queries = queries_ref[head, queries_at, :]
        lanes = slice(head // 2 * 128, head // 2 * 128 + 128)
        for r in range(0, rows, tile):
            waiting.append((head, r, dot(keys_ref[r : r + tile, lanes], queries, (1, 1))))
            if len(waiting) > 2:
                finish(*waiting.pop(0))
    for item in waiting:
        finish(*item)

    @pl.when(jnp.max(sum(wrong)) > 0.0)
    def _():
        def body(i, carry):
            head, part = i // (span // tile), lax.rem(i, span // tile)
            part_at = pl.ds(pl.multiple_of(at + part * tile, tile), tile)
            lanes = pl.ds(pl.multiple_of(head // 2 * 128, 128), 128)
            scores = dot(keys_ref[:, lanes], queries_ref[head, part_at, :], (1, 1)) * scale
            powers = jnp.exp(scores - jnp.max(scores, axis=0, keepdims=True))
            weights = powers / jnp.sum(powers, axis=0, keepdims=True)
            product = dot(values_ref[head, :head_width, :], weights.astype(BF16))
            head_rows = pl.ds(pl.multiple_of(head * head_width, head_width), head_width)
            columns = pl.ds(pl.multiple_of(into.start + part * tile, tile), tile)
            message_ref[head_rows, columns] = product.astype(BF16)
            return carry

        lax.fori_loop(0, HEADS * (span // tile), body, 0)


def takes_other(place):
    return lax.rem(place // 2, 2) == lax.rem(place, 2)


def partner_kernel(step, two, place_ref, queries_ref, facts_ref, x_ref, *refs):
    other_ref, *refs = refs if two else (None, *refs)
    wk_ref, wvt_ref, message_ref, keys_ref, values_ref = refs
    rows, _ = keys_ref.shape
    linked = jnp.max(facts_ref[step : step + 1, :]) > 0.0

    @pl.when(jnp.logical_not(linked))
    def _():
        message_ref[...] = jnp.zeros_like(message_ref)

    @pl.when(linked)
    def _():
        take = takes_other(place_ref[0])
        project(x_ref, other_ref, take, wk_ref, wvt_ref, keys_ref, values_ref)
        wide = rows // 2

        def body(i, carry):
            at = pl.multiple_of(i * wide, wide)
            attend(queries_ref, at, wide, keys_ref, values_ref, message_ref, pl.ds(at, wide))
            return carry

        lax.fori_loop(0, rows // wide, body, 0)


def last_kernel(
    step, place_ref, queries_ref, facts_ref, x_ref, other_ref, wk_ref, wvt_ref, first_ref,
    second_ref, keys_ref, values_ref, send_ref, message_ref,
):
    half = message_ref.shape[1]
    place = place_ref[0]
    at = pl.multiple_of((1 - lax.rem(place, 2)) * half, half)
    here = pl.ds(at, half)
    linked = jnp.max(facts_ref[step : step + 1, :]) > 0.0
    total = first_ref[:, here].astype(F32) + second_ref[:, here].astype(F32)

    @pl.when(jnp.logical_not(linked))
    def _():
        send_ref[...] = total.astype(BF16)

    @pl.when(linked)
    def _():
        project(x_ref, other_ref, takes_other(place), wk_ref, wvt_ref, keys_ref, values_ref)
        attend(queries_ref, at, half, keys_ref, values_ref, message_ref, pl.ds(0, half))
        total = first_ref[:, here].astype(F32) + second_ref[:, here].astype(F32)
        send_ref[...] = (total + message_ref[...].astype(F32)).astype(BF16)


def own_kernel(
    step, place_ref, queries_ref, facts_ref, keys_ref, values_ref, first_ref, second_ref, keep_ref,
    message_ref,
):
    half = message_ref.shape[1]
    at = pl.multiple_of(lax.rem(place_ref[0], 2) * half, half)
    here = pl.ds(at, half)
    linked = jnp.max(facts_ref[step : step + 1, :]) > 0.0

    @pl.when(jnp.logical_not(linked))
    def _():
        keep_ref[...] = first_ref[:, here].astype(F32) + second_ref[:, here].astype(F32)

    @pl.when(linked)
    def _():
        attend(queries_ref, at, half, keys_ref, values_ref, message_ref, pl.ds(0, half))
        total = first_ref[:, here].astype(F32) + second_ref[:, here].astype(F32)
        keep_ref[...] = total + message_ref[...].astype(F32)


def tail_kernel(
    place_ref, keep_ref, came_ref, x_ref, out_ref, mlp_ref, vectors_ref, mlp_out_ref, result_ref
):
    width, rows = keep_ref.shape
    sub = lax.rem(place_ref[0], 2)
    own_rows = x_ref[pl.ds(pl.multiple_of(sub * rows, rows), rows), :]
    hidden = dot(own_rows, mlp_ref[:width, :]) + vectors_ref[2:3, :]
    summed = (keep_ref[...] + came_ref[...].astype(F32)).astype(BF16)
    projected = dot(summed, out_ref[...], (0, 0)).astype(BF16)
    hidden = hidden + dot(projected, mlp_ref[width:, :])
    centered = hidden - jnp.mean(hidden, axis=1, keepdims=True)
    variance = jnp.mean(centered * centered, axis=1, keepdims=True)
    normed = centered * lax.rsqrt(variance + 1e-05) * vectors_ref[0:1, :] + vectors_ref[1:2, :]
    activated = (0.5 * normed * (1.0 + lax.erf(normed * math.sqrt(0.5)))).astype(BF16)
    updated = dot(activated, mlp_out_ref[...]) + vectors_ref[3:4, :width]
    result_ref[...] = (updated + own_rows.astype(F32)).astype(BF16)


def shape(dims, dtype):
    return jax.ShapeDtypeStruct(dims, dtype)


def cost(flops, moved, exps=0):
    return pl.CostEstimate(flops=flops, bytes_accessed=moved, transcendentals=exps)


def on_device(
    descriptors,
    links,
    qk_weight,
    value_weight,
    out_weight,
    mlp_in,
    mlp_in_bias,
    norm_gain,
    norm_bias,
    mlp_out,
    mlp_out_bias,
):
    own = descriptors[0]
    rows, width = own.shape
    hidden_width = mlp_in.shape[1]
    half = rows // 2
    images = lax.axis_size(("img", "pair"))
    place = lax.axis_index(RING).reshape(1)
    params = pltpu.CompilerParams(vmem_limit_bytes=40 << 20)

    swap = [(0, 1), (1, 0)]
    qk_other = lax.ppermute(qk_weight, "sub", swap)
    value_other = lax.ppermute(value_weight, "sub", swap)

    def carried(value, moves):
        pairs = []
        for image in range(images):
            for sub in range(2):
                source = moves(image, sub)
                if source is not None:
                    pairs.append((2 * source[0] + source[1], 2 * image + sub))
        return lax.ppermute(value, RING, pairs)

    def ahead(image, sub, step):
        partner = image + step if sub == 0 else image - step
        return partner if 0 <= partner < images else None

    def by_two(image, sub):
        partner = ahead(image, sub, 2)
        return None if partner is None else (partner, sub)

    def within(image, sub):
        return (image ^ 1, image % 2) if image % 2 == sub else None

    def across(image, sub):
        partner = ahead(image, sub, 1)
        return None if image % 2 == sub or partner is None else (image ^ 1, sub)

    def onward(image, sub):
        return None if ahead(image, sub, 3) is None else (ahead(image, sub, 2), sub)

    def onward_inner(image, sub):
        return onward(image, sub) if image % 2 == sub else None

    def onward_outer(image, sub):
        return None if image % 2 == sub else onward(image, sub)

    two = carried(own, by_two)

    def called(kernel, args, out_shape, scratch, cost_estimate, scalars=1):
        return pl.pallas_call(
            kernel,
            in_specs=[SMEM] * scalars + [VMEM] * (len(args) - scalars),
            out_specs=[VMEM] * len(out_shape),
            out_shape=out_shape,
            scratch_shapes=scratch,
            compiler_params=params,
            cost_estimate=cost_estimate,
        )(*args)

    wk, wvt, queries, facts, vectors = called(
        functools.partial(prologue_kernel, images),
        [
            place, links.T, own, qk_weight, value_weight, qk_other, value_other,
            norm_gain.reshape(1, -1), norm_bias.reshape(1, -1), mlp_in_bias.reshape(1, -1),
            mlp_out_bias.reshape(1, -1),
        ],
        [
            shape((width, width), BF16),
            shape((width, width), BF16),
            shape((HEADS, rows, 128), BF16),
            shape((8, 128), F32),
            shape((8, hidden_width), F32),
        ],
        [],
        cost(4 * rows * width * width, 4 << 20),
        scalars=2,
    )

    own_later, facts = lax.optimization_barrier((own, facts))
    inner = carried(own_later, within)
    outer = carried(two, across)
    projected = [
        shape((rows, width), BF16),
        shape((HEADS, width // HEADS + 16, rows), BF16),
    ]
    scratch = [pltpu.VMEM(x.shape, x.dtype) for x in projected]
    message = [shape((width, rows), BF16)]
    work = cost(8 * rows * rows * width, 2 << 20, HEADS * rows * rows)
    half_work = cost(4 * rows * rows * width, 2 << 20, HEADS * rows * half)
    (message_two,) = called(
        functools.partial(partner_kernel, 2, False),
        [place, queries, facts, two, wk, wvt],
        message,
        scratch,
        work,
    )
    outer, inner, message_two = lax.optimization_barrier((outer, inner, message_two))
    outer_far = carried(outer, onward_outer)
    inner_far = carried(inner, onward_inner)
    (message_one,) = called(
        functools.partial(partner_kernel, 1, True),
        [place, queries, facts, outer, inner, wk, wvt],
        message,
        scratch,
        work,
    )
    inner_far, outer_far, message_one = lax.optimization_barrier(
        (inner_far, outer_far, message_one)
    )
    keys, values, send = called(
        functools.partial(last_kernel, 3),
        [place, queries, facts, outer_far, inner_far, wk, wvt, message_two, message_one],
        [*projected, shape((width, half), BF16)],
        [pltpu.VMEM((width, half), BF16)],
        half_work,
    )
    came = lax.ppermute(send, "sub", swap)
    (keep,) = called(
        functools.partial(own_kernel, 3),
        [place, queries, facts, keys, values, message_two, message_one],
        [shape((width, half), F32)],
        [pltpu.VMEM((width, half), BF16)],
        half_work,
    )
    came, keep = lax.optimization_barrier((came, keep))
    (result,) = called(
        tail_kernel,
        [place, keep, came, own, out_weight, mlp_in, vectors, mlp_out],
        [shape((half, width), BF16)],
        [],
        cost(4 * rows * width * width, 4 << 20),
    )
    return result[None]


def solution(mesh):
    placed = (
        P(("groups", "img", "pair"), None, None),
        P("groups", None),
        P(None, "sub"),
        P(None, "sub"),
        P(),
        P(),
        P(),
        P(),
        P(),
        P(),
        P(),
    )

    return jax.shard_map(
        on_device,
        mesh=mesh,
        in_specs=placed,
        out_specs=P(("groups", "img", "pair"), "sub", None),
        check_vma=False,
    )
```

```python
import functools
import math

import jax
import jax.numpy as jnp
from jax import lax
from jax.experimental import pallas as pl
from jax.experimental.pallas import tpu as pltpu
from jax.sharding import PartitionSpec as P


HEADS = 4
SPAN = 3
RING = ("img", "pair", "sub")
LEAST_SUM, LARGEST_SUM = 1e-20, 1e20
LARGEST_PRODUCT = 1e37
F32 = jnp.float32
BF16 = jnp.bfloat16
VMEM = pl.BlockSpec(memory_space=pltpu.VMEM)
SMEM = pl.BlockSpec(memory_space=pltpu.SMEM)


def dot(a, b, contract=(1, 0)):
    return lax.dot_general(
        a, b, (((contract[0],), (contract[1],)), ((), ())), preferred_element_type=F32
    )


def prologue_kernel(
    images, place_ref, links_ref, x_ref, qk_ref, value_ref, qk_other_ref, value_other_ref, gain_ref,
    shift_ref, bias_ref, out_bias_ref, wk_ref, wvt_ref, queries_ref, facts_ref, rows_ref, vectors_ref,
):
    rows, width = x_ref.shape
    local = width // 2
    sub = lax.rem(place_ref[0], 2)
    image = place_ref[0] // 2
    parts = []
    for own_ref, other_ref in ((qk_ref, qk_other_ref), (value_ref, value_other_ref)):
        own, other = own_ref[...], other_ref[...]
        parts.append(jnp.where(sub == 0, own, other))
        parts.append(jnp.where(sub == 0, other, own))
    wk_ref[:, :local], wk_ref[:, local:] = parts[0], parts[1]
    wvt_ref[:local, :], wvt_ref[local:, :] = parts[2].T, parts[3].T
    keys = dot(x_ref[...], wk_ref[...]).astype(BF16)
    lane = lax.broadcasted_iota(jnp.int32, (rows, 128), 1)
    for head in range(HEADS):
        block, odd = head // 2 * 128, head % 2
        mine = (lane >= 64) if odd else (lane < 64)
        queries_ref[head] = jnp.where(mine, keys[:, block : block + 128], jnp.zeros((), BF16))
    for step in range(1, SPAN + 1):
        lower = image - sub * step
        inside = jnp.logical_and(lower >= 0, lower + step < images)
        entry = links_ref[step - 1, jnp.clip(lower, 0, images - 1)]
        linked = jnp.where(jnp.logical_and(inside, entry != 0), 1.0, 0.0)
        facts_ref[step : step + 1, :] = jnp.full((1, 128), linked, F32)
    half = rows // 2
    rows_ref[...] = x_ref[pl.ds(pl.multiple_of(sub * half, half), half), :]
    vectors_ref[0:1, :] = gain_ref[...]
    vectors_ref[1:2, :] = shift_ref[...]
    vectors_ref[2:3, :] = bias_ref[...]
    vectors_ref[3:4, :width] = out_bias_ref[...]


def project(x_ref, wk_ref, wvt_ref, keys_ref, values_ref):
    rows, width = keys_ref.shape
    head_width = width // HEADS
    tile = 256
    for r in range(0, rows, tile):
        x = x_ref[r : r + tile, :]
        keys_ref[r : r + tile, :] = dot(x, wk_ref[...]).astype(BF16)
        values = dot(wvt_ref[...], x, (1, 1)).astype(BF16)
        for head in range(HEADS):
            values_ref[head, :head_width, r : r + tile] = values[
                head * head_width : (head + 1) * head_width, :
            ]
            values_ref[head, head_width:, r : r + tile] = jnp.ones((16, tile), BF16)


def attend(queries_ref, at, span, keys_ref, values_ref, message_ref, into):
    rows, width = keys_ref.shape
    head_width = width // HEADS
    scale = 1.0 / math.sqrt(head_width)
    tile = 256
    queries_at = pl.ds(pl.multiple_of(at, span), span)
    totals = {}
    wrong = []

    def finish(head, r, scores):
        weights = jnp.exp2(scores * (scale * math.log2(math.e))).astype(BF16)
        product = dot(values_ref[head, :, r : r + tile], weights)
        total = product if r == 0 else totals[head] + product
        totals[head] = total
        if r + tile == rows:
            sums = total[head_width : head_width + 1]
            message_ref[head * head_width : (head + 1) * head_width, into] = (
                total[:head_width] * (1.0 / sums)
            ).astype(BF16)
            top = jnp.max(jnp.abs(total[:head_width]), axis=0, keepdims=True)
            fine = jnp.logical_and(sums > LEAST_SUM, sums < LARGEST_SUM)
            fine = jnp.logical_and(fine, top < LARGEST_PRODUCT)
            wrong.append(jnp.where(fine, 0.0, 1.0))

    waiting = []
    for head in range(HEADS):
        queries = queries_ref[head, queries_at, :]
        lanes = slice(head // 2 * 128, head // 2 * 128 + 128)
        for r in range(0, rows, tile):
            waiting.append((head, r, dot(keys_ref[r : r + tile, lanes], queries, (1, 1))))
            if len(waiting) > 2:
                finish(*waiting.pop(0))
    for item in waiting:
        finish(*item)

    @pl.when(jnp.max(sum(wrong)) > 0.0)
    def _():
        def body(i, carry):
            head, part = i // (span // tile), lax.rem(i, span // tile)
            part_at = pl.ds(pl.multiple_of(at + part * tile, tile), tile)
            lanes = pl.ds(pl.multiple_of(head // 2 * 128, 128), 128)
            scores = dot(keys_ref[:, lanes], queries_ref[head, part_at, :], (1, 1)) * scale
            powers = jnp.exp(scores - jnp.max(scores, axis=0, keepdims=True))
            weights = powers / jnp.sum(powers, axis=0, keepdims=True)
            product = dot(values_ref[head, :head_width, :], weights.astype(BF16))
            head_rows = pl.ds(pl.multiple_of(head * head_width, head_width), head_width)
            columns = pl.ds(pl.multiple_of(into.start + part * tile, tile), tile)
            message_ref[head_rows, columns] = product.astype(BF16)
            return carry

        lax.fori_loop(0, HEADS * (span // tile), body, 0)


def partner_kernel(
    step, queries_ref, facts_ref, x_ref, wk_ref, wvt_ref, message_ref, keys_ref, values_ref
):
    rows, _ = keys_ref.shape
    linked = jnp.max(facts_ref[step : step + 1, :]) > 0.0

    @pl.when(jnp.logical_not(linked))
    def _():
        message_ref[...] = jnp.zeros_like(message_ref)

    @pl.when(linked)
    def _():
        project(x_ref, wk_ref, wvt_ref, keys_ref, values_ref)
        wide = rows // 2

        def body(i, carry):
            at = pl.multiple_of(i * wide, wide)
            attend(queries_ref, at, wide, keys_ref, values_ref, message_ref, pl.ds(at, wide))
            return carry

        lax.fori_loop(0, rows // wide, body, 0)


def last_kernel(
    step, place_ref, queries_ref, facts_ref, x_ref, wk_ref, wvt_ref, first_ref, second_ref,
    keys_ref, values_ref, send_ref, message_ref,
):
    half = message_ref.shape[1]
    place = place_ref[0]
    at = pl.multiple_of((1 - lax.rem(place, 2)) * half, half)
    here = pl.ds(at, half)
    linked = jnp.max(facts_ref[step : step + 1, :]) > 0.0
    total = first_ref[:, here].astype(F32) + second_ref[:, here].astype(F32)

    @pl.when(jnp.logical_not(linked))
    def _():
        send_ref[...] = total.astype(BF16)

    @pl.when(linked)
    def _():
        project(x_ref, wk_ref, wvt_ref, keys_ref, values_ref)
        attend(queries_ref, at, half, keys_ref, values_ref, message_ref, pl.ds(0, half))
        total = first_ref[:, here].astype(F32) + second_ref[:, here].astype(F32)
        send_ref[...] = (total + message_ref[...].astype(F32)).astype(BF16)


def own_kernel(
    step, place_ref, queries_ref, facts_ref, keys_ref, values_ref, first_ref, second_ref, keep_ref,
    message_ref,
):
    half = message_ref.shape[1]
    at = pl.multiple_of(lax.rem(place_ref[0], 2) * half, half)
    here = pl.ds(at, half)
    linked = jnp.max(facts_ref[step : step + 1, :]) > 0.0

    @pl.when(jnp.logical_not(linked))
    def _():
        keep_ref[...] = first_ref[:, here].astype(F32) + second_ref[:, here].astype(F32)

    @pl.when(linked)
    def _():
        attend(queries_ref, at, half, keys_ref, values_ref, message_ref, pl.ds(0, half))
        total = first_ref[:, here].astype(F32) + second_ref[:, here].astype(F32)
        keep_ref[...] = total + message_ref[...].astype(F32)


def tail_kernel(
    keep_ref, came_ref, rows_ref, out_ref, mlp_ref, vectors_ref, mlp_out_ref, result_ref
):
    width = keep_ref.shape[0]
    own_rows = rows_ref[...]
    hidden = dot(own_rows, mlp_ref[:width, :]) + vectors_ref[2:3, :]
    summed = (keep_ref[...] + came_ref[...].astype(F32)).astype(BF16)
    projected = dot(summed, out_ref[...], (0, 0)).astype(BF16)
    hidden = hidden + dot(projected, mlp_ref[width:, :])
    centered = hidden - jnp.mean(hidden, axis=1, keepdims=True)
    variance = jnp.mean(centered * centered, axis=1, keepdims=True)
    normed = centered * lax.rsqrt(variance + 1e-05) * vectors_ref[0:1, :] + vectors_ref[1:2, :]
    activated = (0.5 * normed * (1.0 + lax.erf(normed * math.sqrt(0.5)))).astype(BF16)
    updated = dot(activated, mlp_out_ref[...]) + vectors_ref[3:4, :width]
    result_ref[...] = (updated + own_rows.astype(F32)).astype(BF16)


def shape(dims, dtype):
    return jax.ShapeDtypeStruct(dims, dtype)


def cost(flops, moved, exps=0):
    return pl.CostEstimate(flops=flops, bytes_accessed=moved, transcendentals=exps)


def on_device(
    descriptors,
    links,
    qk_weight,
    value_weight,
    out_weight,
    mlp_in,
    mlp_in_bias,
    norm_gain,
    norm_bias,
    mlp_out,
    mlp_out_bias,
):
    own = descriptors[0]
    rows, width = own.shape
    hidden_width = mlp_in.shape[1]
    half = rows // 2
    images = lax.axis_size(("img", "pair"))
    place = lax.axis_index(RING).reshape(1)
    params = pltpu.CompilerParams(vmem_limit_bytes=40 << 20)

    swap = [(0, 1), (1, 0)]
    qk_other = lax.ppermute(qk_weight, "sub", swap)
    value_other = lax.ppermute(value_weight, "sub", swap)

    def fetched(step):
        pairs = []
        for image in range(images):
            if image >= step:
                pairs.append((2 * image, 2 * (image - step)))
            if image + step < images:
                pairs.append((2 * image + 1, 2 * (image + step) + 1))
        return lax.ppermute(own, RING, pairs)

    three, two, one = (fetched(step) for step in (3, 2, 1))

    def called(kernel, args, out_shape, scratch, cost_estimate, scalars=1):
        return pl.pallas_call(
            kernel,
            in_specs=[SMEM] * scalars + [VMEM] * (len(args) - scalars),
            out_specs=[VMEM] * len(out_shape),
            out_shape=out_shape,
            scratch_shapes=scratch,
            compiler_params=params,
            cost_estimate=cost_estimate,
        )(*args)

    wk, wvt, queries, facts, own_half, vectors = called(
        functools.partial(prologue_kernel, images),
        [
            place, links.T, own, qk_weight, value_weight, qk_other, value_other,
            norm_gain.reshape(1, -1), norm_bias.reshape(1, -1), mlp_in_bias.reshape(1, -1),
            mlp_out_bias.reshape(1, -1),
        ],
        [
            shape((width, width), BF16),
            shape((width, width), BF16),
            shape((HEADS, rows, 128), BF16),
            shape((8, 128), F32),
            shape((half, width), BF16),
            shape((8, hidden_width), F32),
        ],
        [],
        cost(4 * rows * width * width, 4 << 20),
        scalars=2,
    )

    projected = [
        shape((rows, width), BF16),
        shape((HEADS, width // HEADS + 16, rows), BF16),
    ]
    scratch = [pltpu.VMEM(x.shape, x.dtype) for x in projected]
    message = [shape((width, rows), BF16)]
    work = cost(8 * rows * rows * width, 2 << 20, HEADS * rows * rows)
    half_work = cost(4 * rows * rows * width, 2 << 20, HEADS * rows * half)
    messages = []
    for step, partner in ((3, three), (2, two)):
        if messages:
            partner, messages = lax.optimization_barrier((partner, messages))
        messages += called(
            functools.partial(partner_kernel, step),
            [queries, facts, partner, wk, wvt],
            message,
            scratch,
            work,
            scalars=0,
        )
    one, messages = lax.optimization_barrier((one, messages))
    keys, values, send = called(
        functools.partial(last_kernel, 1),
        [place, queries, facts, one, wk, wvt, *messages],
        [*projected, shape((width, half), BF16)],
        [pltpu.VMEM((width, half), BF16)],
        half_work,
    )
    came = lax.ppermute(send, "sub", swap)
    (keep,) = called(
        functools.partial(own_kernel, 1),
        [place, queries, facts, keys, values, *messages],
        [shape((width, half), F32)],
        [pltpu.VMEM((width, half), BF16)],
        half_work,
    )
    came, keep = lax.optimization_barrier((came, keep))
    (result,) = called(
        tail_kernel,
        [keep, came, own_half, out_weight, mlp_in, vectors, mlp_out],
        [shape((half, width), BF16)],
        [],
        cost(4 * rows * width * width, 4 << 20),
        scalars=0,
    )
    return result[None]


def solution(mesh):
    placed = (
        P(("groups", "img", "pair"), None, None),
        P("groups", None),
        P(None, "sub"),
        P(None, "sub"),
        P(),
        P(),
        P(),
        P(),
        P(),
        P(),
        P(),
    )

    return jax.shard_map(
        on_device,
        mesh=mesh,
        in_specs=placed,
        out_specs=P(("groups", "img", "pair"), "sub", None),
        check_vma=False,
    )
```

```python
import functools
import math

import jax
import jax.numpy as jnp
from jax import lax
from jax.experimental import pallas as pl
from jax.experimental.pallas import tpu as pltpu
from jax.sharding import PartitionSpec as P


HEADS = 4
SPAN = 3
RING = ("img", "pair", "sub")
LEAST_SUM, LARGEST_SUM = 1e-20, 1e20
LARGEST_PRODUCT = 1e37
F32 = jnp.float32
BF16 = jnp.bfloat16
VMEM = pl.BlockSpec(memory_space=pltpu.VMEM)
SMEM = pl.BlockSpec(memory_space=pltpu.SMEM)


def dot(a, b, contract=(1, 0)):
    return lax.dot_general(
        a, b, (((contract[0],), (contract[1],)), ((), ())), preferred_element_type=F32
    )


def prologue_kernel(
    images, place_ref, links_ref, x_ref, qk_ref, value_ref, qk_other_ref, value_other_ref, gain_ref,
    shift_ref, bias_ref, out_bias_ref, wk_ref, wvt_ref, queries_ref, facts_ref, rows_ref, vectors_ref,
):
    rows, width = x_ref.shape
    local = width // 2
    sub = lax.rem(place_ref[0], 2)
    image = place_ref[0] // 2
    parts = []
    for own_ref, other_ref in ((qk_ref, qk_other_ref), (value_ref, value_other_ref)):
        own, other = own_ref[...], other_ref[...]
        parts.append(jnp.where(sub == 0, own, other))
        parts.append(jnp.where(sub == 0, other, own))
    wk_ref[:, :local], wk_ref[:, local:] = parts[0], parts[1]
    wvt_ref[:local, :], wvt_ref[local:, :] = parts[2].T, parts[3].T
    keys = dot(x_ref[...], wk_ref[...]).astype(BF16)
    lane = lax.broadcasted_iota(jnp.int32, (rows, 128), 1)
    for head in range(HEADS):
        block, odd = head // 2 * 128, head % 2
        mine = (lane >= 64) if odd else (lane < 64)
        queries_ref[head] = jnp.where(mine, keys[:, block : block + 128], jnp.zeros((), BF16))
    for step in range(1, SPAN + 1):
        lower = image - sub * step
        inside = jnp.logical_and(lower >= 0, lower + step < images)
        entry = links_ref[step - 1, jnp.clip(lower, 0, images - 1)]
        linked = jnp.where(jnp.logical_and(inside, entry != 0), 1.0, 0.0)
        facts_ref[step : step + 1, :] = jnp.full((1, 128), linked, F32)
    half = rows // 2
    rows_ref[...] = x_ref[pl.ds(pl.multiple_of(sub * half, half), half), :]
    vectors_ref[0:1, :] = gain_ref[...]
    vectors_ref[1:2, :] = shift_ref[...]
    vectors_ref[2:3, :] = bias_ref[...]
    vectors_ref[3:4, :width] = out_bias_ref[...]


def project(x_ref, other_ref, take_other, wk_ref, wvt_ref, keys_ref, values_ref):
    rows, width = keys_ref.shape
    head_width = width // HEADS
    tile = 256
    for r in range(0, rows, tile):
        x = x_ref[r : r + tile, :]
        if other_ref is not None:
            x = jnp.where(take_other, other_ref[r : r + tile, :], x)
        keys_ref[r : r + tile, :] = dot(x, wk_ref[...]).astype(BF16)
        values = dot(wvt_ref[...], x, (1, 1)).astype(BF16)
        for head in range(HEADS):
            values_ref[head, :head_width, r : r + tile] = values[
                head * head_width : (head + 1) * head_width, :
            ]
            values_ref[head, head_width:, r : r + tile] = jnp.ones((16, tile), BF16)


def attend(queries_ref, at, span, keys_ref, values_ref, message_ref, into):
    rows, width = keys_ref.shape
    head_width = width // HEADS
    scale = 1.0 / math.sqrt(head_width)
    tile = 256
    queries_at = pl.ds(pl.multiple_of(at, span), span)
    totals = {}
    wrong = []

    def finish(head, r, scores):
        weights = jnp.exp2(scores * (scale * math.log2(math.e))).astype(BF16)
        product = dot(values_ref[head, :, r : r + tile], weights)
        total = product if r == 0 else totals[head] + product
        totals[head] = total
        if r + tile == rows:
            sums = total[head_width : head_width + 1]
            message_ref[head * head_width : (head + 1) * head_width, into] = (
                total[:head_width] * (1.0 / sums)
            ).astype(BF16)
            top = jnp.max(jnp.abs(total[:head_width]), axis=0, keepdims=True)
            fine = jnp.logical_and(sums > LEAST_SUM, sums < LARGEST_SUM)
            fine = jnp.logical_and(fine, top < LARGEST_PRODUCT)
            wrong.append(jnp.where(fine, 0.0, 1.0))

    waiting = []
    for head in range(HEADS):
        queries = queries_ref[head, queries_at, :]
        lanes = slice(head // 2 * 128, head // 2 * 128 + 128)
        for r in range(0, rows, tile):
            waiting.append((head, r, dot(keys_ref[r : r + tile, lanes], queries, (1, 1))))
            if len(waiting) > 2:
                finish(*waiting.pop(0))
    for item in waiting:
        finish(*item)

    @pl.when(jnp.max(sum(wrong)) > 0.0)
    def _():
        def body(i, carry):
            head, part = i // (span // tile), lax.rem(i, span // tile)
            part_at = pl.ds(pl.multiple_of(at + part * tile, tile), tile)
            lanes = pl.ds(pl.multiple_of(head // 2 * 128, 128), 128)
            scores = dot(keys_ref[:, lanes], queries_ref[head, part_at, :], (1, 1)) * scale
            powers = jnp.exp(scores - jnp.max(scores, axis=0, keepdims=True))
            weights = powers / jnp.sum(powers, axis=0, keepdims=True)
            product = dot(values_ref[head, :head_width, :], weights.astype(BF16))
            head_rows = pl.ds(pl.multiple_of(head * head_width, head_width), head_width)
            columns = pl.ds(pl.multiple_of(into.start + part * tile, tile), tile)
            message_ref[head_rows, columns] = product.astype(BF16)
            return carry

        lax.fori_loop(0, HEADS * (span // tile), body, 0)


def near_first(place):
    return lax.rem(place // 2, 2) == lax.rem(place, 2)


def partner_kernel(step, two, place_ref, queries_ref, facts_ref, x_ref, *refs):
    other_ref, *refs = refs if two else (None, *refs)
    wk_ref, wvt_ref, message_ref, keys_ref, values_ref = refs
    rows, _ = keys_ref.shape
    linked = jnp.max(facts_ref[step : step + 1, :]) > 0.0

    @pl.when(jnp.logical_not(linked))
    def _():
        message_ref[...] = jnp.zeros_like(message_ref)

    @pl.when(linked)
    def _():
        take = near_first(place_ref[0])
        project(x_ref, other_ref, take, wk_ref, wvt_ref, keys_ref, values_ref)
        wide = rows // 2

        def body(i, carry):
            at = pl.multiple_of(i * wide, wide)
            attend(queries_ref, at, wide, keys_ref, values_ref, message_ref, pl.ds(at, wide))
            return carry

        lax.fori_loop(0, rows // wide, body, 0)


def last_kernel(
    step, place_ref, queries_ref, facts_ref, x_ref, other_ref, wk_ref, wvt_ref, first_ref,
    second_ref, keys_ref, values_ref, send_ref, message_ref,
):
    half = message_ref.shape[1]
    place = place_ref[0]
    at = pl.multiple_of((1 - lax.rem(place, 2)) * half, half)
    here = pl.ds(at, half)
    linked = jnp.max(facts_ref[step : step + 1, :]) > 0.0
    total = first_ref[:, here].astype(F32) + second_ref[:, here].astype(F32)

    @pl.when(jnp.logical_not(linked))
    def _():
        send_ref[...] = total.astype(BF16)

    @pl.when(linked)
    def _():
        project(x_ref, other_ref, near_first(place), wk_ref, wvt_ref, keys_ref, values_ref)
        attend(queries_ref, at, half, keys_ref, values_ref, message_ref, pl.ds(0, half))
        total = first_ref[:, here].astype(F32) + second_ref[:, here].astype(F32)
        send_ref[...] = (total + message_ref[...].astype(F32)).astype(BF16)


def own_kernel(
    step, place_ref, queries_ref, facts_ref, keys_ref, values_ref, first_ref, second_ref, keep_ref,
    message_ref,
):
    half = message_ref.shape[1]
    at = pl.multiple_of(lax.rem(place_ref[0], 2) * half, half)
    here = pl.ds(at, half)
    linked = jnp.max(facts_ref[step : step + 1, :]) > 0.0

    @pl.when(jnp.logical_not(linked))
    def _():
        keep_ref[...] = first_ref[:, here].astype(F32) + second_ref[:, here].astype(F32)

    @pl.when(linked)
    def _():
        attend(queries_ref, at, half, keys_ref, values_ref, message_ref, pl.ds(0, half))
        total = first_ref[:, here].astype(F32) + second_ref[:, here].astype(F32)
        keep_ref[...] = total + message_ref[...].astype(F32)


def tail_kernel(
    keep_ref, came_ref, rows_ref, out_ref, mlp_ref, vectors_ref, mlp_out_ref, result_ref
):
    width = keep_ref.shape[0]
    own_rows = rows_ref[...]
    hidden = dot(own_rows, mlp_ref[:width, :]) + vectors_ref[2:3, :]
    summed = (keep_ref[...] + came_ref[...].astype(F32)).astype(BF16)
    projected = dot(summed, out_ref[...], (0, 0)).astype(BF16)
    hidden = hidden + dot(projected, mlp_ref[width:, :])
    centered = hidden - jnp.mean(hidden, axis=1, keepdims=True)
    variance = jnp.mean(centered * centered, axis=1, keepdims=True)
    normed = centered * lax.rsqrt(variance + 1e-05) * vectors_ref[0:1, :] + vectors_ref[1:2, :]
    activated = (0.5 * normed * (1.0 + lax.erf(normed * math.sqrt(0.5)))).astype(BF16)
    updated = dot(activated, mlp_out_ref[...]) + vectors_ref[3:4, :width]
    result_ref[...] = (updated + own_rows.astype(F32)).astype(BF16)


def shape(dims, dtype):
    return jax.ShapeDtypeStruct(dims, dtype)


def cost(flops, moved, exps=0):
    return pl.CostEstimate(flops=flops, bytes_accessed=moved, transcendentals=exps)


def on_device(
    descriptors,
    links,
    qk_weight,
    value_weight,
    out_weight,
    mlp_in,
    mlp_in_bias,
    norm_gain,
    norm_bias,
    mlp_out,
    mlp_out_bias,
):
    own = descriptors[0]
    rows, width = own.shape
    hidden_width = mlp_in.shape[1]
    half = rows // 2
    images = lax.axis_size(("img", "pair"))
    place = lax.axis_index(RING).reshape(1)
    params = pltpu.CompilerParams(vmem_limit_bytes=40 << 20)

    swap = [(0, 1), (1, 0)]
    qk_other = lax.ppermute(qk_weight, "sub", swap)
    value_other = lax.ppermute(value_weight, "sub", swap)

    def carried(value, source):
        pairs = []
        for image in range(images):
            for sub in range(2):
                origin = source(image, sub)
                if origin is not None:
                    pairs.append((2 * origin[0] + origin[1], 2 * image + sub))
        return lax.ppermute(value, RING, pairs)

    def ahead(image, sub, step):
        partner = image + step if sub == 0 else image - step
        return partner if 0 <= partner < images else None

    def near(image, sub):
        return image % 2 == sub

    def within(image, sub):
        return (image ^ 1, image % 2) if near(image, sub) else None

    def by_two(image, sub):
        partner = ahead(image, sub, 2)
        return None if partner is None else (partner, sub)

    def outer(image, sub):
        partner = ahead(image, sub, 1)
        return None if near(image, sub) or partner is None else (partner, 1 - sub)

    def far_outer(image, sub):
        partner = ahead(image, sub, 3)
        if near(image, sub) or partner is None:
            return None
        return (partner ^ 1, (partner ^ 1) % 2)

    def far_inner(image, sub):
        if not near(image, sub) or ahead(image, sub, 3) is None:
            return None
        return (ahead(image, sub, 2), sub)

    one_inner = carried(own, within)
    two = carried(own, by_two)
    one_outer = carried(own, outer)

    def called(kernel, args, out_shape, scratch, cost_estimate, scalars=1):
        return pl.pallas_call(
            kernel,
            in_specs=[SMEM] * scalars + [VMEM] * (len(args) - scalars),
            out_specs=[VMEM] * len(out_shape),
            out_shape=out_shape,
            scratch_shapes=scratch,
            compiler_params=params,
            cost_estimate=cost_estimate,
        )(*args)

    wk, wvt, queries, facts, own_half, vectors = called(
        functools.partial(prologue_kernel, images),
        [
            place, links.T, own, qk_weight, value_weight, qk_other, value_other,
            norm_gain.reshape(1, -1), norm_bias.reshape(1, -1), mlp_in_bias.reshape(1, -1),
            mlp_out_bias.reshape(1, -1),
        ],
        [
            shape((width, width), BF16),
            shape((width, width), BF16),
            shape((HEADS, rows, 128), BF16),
            shape((8, 128), F32),
            shape((half, width), BF16),
            shape((8, hidden_width), F32),
        ],
        [],
        cost(4 * rows * width * width, 4 << 20),
        scalars=2,
    )

    one_inner, facts = lax.optimization_barrier((one_inner, facts))
    three_outer = carried(one_inner, far_outer)
    three_inner = carried(one_inner, far_inner)

    projected = [
        shape((rows, width), BF16),
        shape((HEADS, width // HEADS + 16, rows), BF16),
    ]
    scratch = [pltpu.VMEM(x.shape, x.dtype) for x in projected]
    message_shape = [shape((width, rows), BF16)]
    work = cost(8 * rows * rows * width, 2 << 20, HEADS * rows * rows)
    half_work = cost(4 * rows * rows * width, 2 << 20, HEADS * rows * half)
    (message,) = called(
        functools.partial(partner_kernel, 2, False),
        [place, queries, facts, two, wk, wvt],
        message_shape,
        scratch,
        work,
    )
    one_outer, message = lax.optimization_barrier((one_outer, message))
    messages = [message]
    messages += called(
        functools.partial(partner_kernel, 1, True),
        [place, queries, facts, one_outer, one_inner, wk, wvt],
        message_shape,
        scratch,
        work,
    )
    three_outer, three_inner, messages = lax.optimization_barrier(
        (three_outer, three_inner, messages)
    )
    keys, values, send = called(
        functools.partial(last_kernel, 3),
        [place, queries, facts, three_outer, three_inner, wk, wvt, *messages],
        [*projected, shape((width, half), BF16)],
        [pltpu.VMEM((width, half), BF16)],
        half_work,
    )
    came = lax.ppermute(send, "sub", swap)
    (keep,) = called(
        functools.partial(own_kernel, 3),
        [place, queries, facts, keys, values, *messages],
        [shape((width, half), F32)],
        [pltpu.VMEM((width, half), BF16)],
        half_work,
    )
    came, keep = lax.optimization_barrier((came, keep))
    (result,) = called(
        tail_kernel,
        [keep, came, own_half, out_weight, mlp_in, vectors, mlp_out],
        [shape((half, width), BF16)],
        [],
        cost(4 * rows * width * width, 4 << 20),
        scalars=0,
    )
    return result[None]


def solution(mesh):
    placed = (
        P(("groups", "img", "pair"), None, None),
        P("groups", None),
        P(None, "sub"),
        P(None, "sub"),
        P(),
        P(),
        P(),
        P(),
        P(),
        P(),
        P(),
    )

    return jax.shard_map(
        on_device,
        mesh=mesh,
        in_specs=placed,
        out_specs=P(("groups", "img", "pair"), "sub", None),
        check_vma=False,
    )
```

```python
import functools
import math

import jax
import jax.numpy as jnp
from jax import lax
from jax.experimental import pallas as pl
from jax.experimental.pallas import tpu as pltpu
from jax.sharding import PartitionSpec as P


HEADS = 4
SPAN = 3
RING = ("img", "pair", "sub")
LEAST_SUM, LARGEST_SUM = 1e-20, 1e20
LARGEST_PRODUCT = 1e37
F32 = jnp.float32
BF16 = jnp.bfloat16
VMEM = pl.BlockSpec(memory_space=pltpu.VMEM)
SMEM = pl.BlockSpec(memory_space=pltpu.SMEM)


def dot(a, b, contract=(1, 0)):
    return lax.dot_general(
        a, b, (((contract[0],), (contract[1],)), ((), ())), preferred_element_type=F32
    )


def prologue_kernel(
    images, place_ref, links_ref, x_ref, own_ref, qk_other_ref, value_other_ref, gain_ref,
    shift_ref, bias_ref, out_bias_ref, wk_ref, wvt_ref, queries_ref, facts_ref, rows_ref, vectors_ref,
):
    rows, width = x_ref.shape
    local = width // 2
    sub = lax.rem(place_ref[0], 2)
    image = place_ref[0] // 2
    parts = []
    for i, other_ref in enumerate((qk_other_ref, value_other_ref)):
        own, other = own_ref[:, i * local : (i + 1) * local], other_ref[...]
        parts.append(jnp.where(sub == 0, own, other))
        parts.append(jnp.where(sub == 0, other, own))
    wk_ref[:, :local], wk_ref[:, local:] = parts[0], parts[1]
    wvt_ref[:local, :], wvt_ref[local:, :] = parts[2].T, parts[3].T
    keys = dot(x_ref[...], wk_ref[...]).astype(BF16)
    lane = lax.broadcasted_iota(jnp.int32, (rows, 128), 1)
    for head in range(HEADS):
        block, odd = head // 2 * 128, head % 2
        mine = (lane >= 64) if odd else (lane < 64)
        queries_ref[head] = jnp.where(mine, keys[:, block : block + 128], jnp.zeros((), BF16))
    for step in range(1, SPAN + 1):
        lower = image - sub * step
        inside = jnp.logical_and(lower >= 0, lower + step < images)
        entry = links_ref[step - 1, jnp.clip(lower, 0, images - 1)]
        linked = jnp.where(jnp.logical_and(inside, entry != 0), 1.0, 0.0)
        facts_ref[step : step + 1, :] = jnp.full((1, 128), linked, F32)
    half = rows // 2
    rows_ref[...] = x_ref[pl.ds(pl.multiple_of(sub * half, half), half), :]
    vectors_ref[0:1, :] = gain_ref[...]
    vectors_ref[1:2, :] = shift_ref[...]
    vectors_ref[2:3, :] = bias_ref[...]
    vectors_ref[3:4, :width] = out_bias_ref[...]


def project(x_ref, other_ref, take_other, wk_ref, wvt_ref, keys_ref, values_ref):
    rows, width = keys_ref.shape
    head_width = width // HEADS
    tile = 256
    for r in range(0, rows, tile):
        x = x_ref[r : r + tile, :]
        if other_ref is not None:
            x = jnp.where(take_other, other_ref[r : r + tile, :], x)
        keys_ref[r : r + tile, :] = dot(x, wk_ref[...]).astype(BF16)
        values = dot(wvt_ref[...], x, (1, 1)).astype(BF16)
        for head in range(HEADS):
            values_ref[head, :head_width, r : r + tile] = values[
                head * head_width : (head + 1) * head_width, :
            ]
            values_ref[head, head_width:, r : r + tile] = jnp.ones((16, tile), BF16)


def attend(queries_ref, at, span, keys_ref, values_ref, message_ref, into):
    rows, width = keys_ref.shape
    head_width = width // HEADS
    scale = 1.0 / math.sqrt(head_width)
    tile = 256
    queries_at = pl.ds(pl.multiple_of(at, span), span)
    totals = {}
    wrong = []

    def finish(head, r, scores):
        weights = jnp.exp2(scores * (scale * math.log2(math.e))).astype(BF16)
        product = dot(values_ref[head, :, r : r + tile], weights)
        total = product if r == 0 else totals[head] + product
        totals[head] = total
        if r + tile == rows:
            sums = total[head_width : head_width + 1]
            message_ref[head * head_width : (head + 1) * head_width, into] = (
                total[:head_width] * (1.0 / sums)
            ).astype(BF16)
            top = jnp.max(jnp.abs(total[:head_width]), axis=0, keepdims=True)
            fine = jnp.logical_and(sums > LEAST_SUM, sums < LARGEST_SUM)
            fine = jnp.logical_and(fine, top < LARGEST_PRODUCT)
            wrong.append(jnp.where(fine, 0.0, 1.0))

    waiting = []
    for head in range(HEADS):
        queries = queries_ref[head, queries_at, :]
        lanes = slice(head // 2 * 128, head // 2 * 128 + 128)
        for r in range(0, rows, tile):
            waiting.append((head, r, dot(keys_ref[r : r + tile, lanes], queries, (1, 1))))
            if len(waiting) > 2:
                finish(*waiting.pop(0))
    for item in waiting:
        finish(*item)

    @pl.when(jnp.max(sum(wrong)) > 0.0)
    def _():
        def body(i, carry):
            head, part = i // (span // tile), lax.rem(i, span // tile)
            part_at = pl.ds(pl.multiple_of(at + part * tile, tile), tile)
            lanes = pl.ds(pl.multiple_of(head // 2 * 128, 128), 128)
            scores = dot(keys_ref[:, lanes], queries_ref[head, part_at, :], (1, 1)) * scale
            powers = jnp.exp(scores - jnp.max(scores, axis=0, keepdims=True))
            weights = powers / jnp.sum(powers, axis=0, keepdims=True)
            product = dot(values_ref[head, :head_width, :], weights.astype(BF16))
            head_rows = pl.ds(pl.multiple_of(head * head_width, head_width), head_width)
            columns = pl.ds(pl.multiple_of(into.start + part * tile, tile), tile)
            message_ref[head_rows, columns] = product.astype(BF16)
            return carry

        lax.fori_loop(0, HEADS * (span // tile), body, 0)


def near_first(place):
    return lax.rem(place // 2, 2) == lax.rem(place, 2)


def partner_kernel(step, two, place_ref, queries_ref, facts_ref, x_ref, *refs):
    other_ref, *refs = refs if two else (None, *refs)
    wk_ref, wvt_ref, message_ref, keys_ref, values_ref = refs
    rows, _ = keys_ref.shape
    linked = jnp.max(facts_ref[step : step + 1, :]) > 0.0

    @pl.when(jnp.logical_not(linked))
    def _():
        message_ref[...] = jnp.zeros_like(message_ref)

    @pl.when(linked)
    def _():
        take = near_first(place_ref[0])
        project(x_ref, other_ref, take, wk_ref, wvt_ref, keys_ref, values_ref)
        wide = rows // 2

        def body(i, carry):
            at = pl.multiple_of(i * wide, wide)
            attend(queries_ref, at, wide, keys_ref, values_ref, message_ref, pl.ds(at, wide))
            return carry

        lax.fori_loop(0, rows // wide, body, 0)


def last_kernel(
    step, place_ref, queries_ref, facts_ref, x_ref, other_ref, wk_ref, wvt_ref, first_ref,
    second_ref, keys_ref, values_ref, send_ref, message_ref,
):
    half = message_ref.shape[1]
    place = place_ref[0]
    at = pl.multiple_of((1 - lax.rem(place, 2)) * half, half)
    here = pl.ds(at, half)
    linked = jnp.max(facts_ref[step : step + 1, :]) > 0.0
    total = first_ref[:, here].astype(F32) + second_ref[:, here].astype(F32)

    @pl.when(jnp.logical_not(linked))
    def _():
        send_ref[...] = total.astype(BF16)

    @pl.when(linked)
    def _():
        project(x_ref, other_ref, near_first(place), wk_ref, wvt_ref, keys_ref, values_ref)
        attend(queries_ref, at, half, keys_ref, values_ref, message_ref, pl.ds(0, half))
        total = first_ref[:, here].astype(F32) + second_ref[:, here].astype(F32)
        send_ref[...] = (total + message_ref[...].astype(F32)).astype(BF16)


def own_kernel(
    step, place_ref, queries_ref, facts_ref, keys_ref, values_ref, first_ref, second_ref, keep_ref,
    message_ref,
):
    half = message_ref.shape[1]
    at = pl.multiple_of(lax.rem(place_ref[0], 2) * half, half)
    here = pl.ds(at, half)
    linked = jnp.max(facts_ref[step : step + 1, :]) > 0.0

    @pl.when(jnp.logical_not(linked))
    def _():
        keep_ref[...] = first_ref[:, here].astype(F32) + second_ref[:, here].astype(F32)

    @pl.when(linked)
    def _():
        attend(queries_ref, at, half, keys_ref, values_ref, message_ref, pl.ds(0, half))
        total = first_ref[:, here].astype(F32) + second_ref[:, here].astype(F32)
        keep_ref[...] = total + message_ref[...].astype(F32)


def tail_kernel(
    keep_ref, came_ref, rows_ref, out_ref, mlp_ref, vectors_ref, mlp_out_ref, result_ref
):
    width = keep_ref.shape[0]
    own_rows = rows_ref[...]
    hidden = dot(own_rows, mlp_ref[:width, :]) + vectors_ref[2:3, :]
    summed = (keep_ref[...] + came_ref[...].astype(F32)).astype(BF16)
    projected = dot(summed, out_ref[...], (0, 0)).astype(BF16)
    hidden = hidden + dot(projected, mlp_ref[width:, :])
    centered = hidden - jnp.mean(hidden, axis=1, keepdims=True)
    variance = jnp.mean(centered * centered, axis=1, keepdims=True)
    normed = centered * lax.rsqrt(variance + 1e-05) * vectors_ref[0:1, :] + vectors_ref[1:2, :]
    activated = (0.5 * normed * (1.0 + lax.erf(normed * math.sqrt(0.5)))).astype(BF16)
    updated = dot(activated, mlp_out_ref[...]) + vectors_ref[3:4, :width]
    result_ref[...] = (updated + own_rows.astype(F32)).astype(BF16)


def shape(dims, dtype):
    return jax.ShapeDtypeStruct(dims, dtype)


def cost(flops, moved, exps=0):
    return pl.CostEstimate(flops=flops, bytes_accessed=moved, transcendentals=exps)


def on_device(
    descriptors,
    links,
    qk_weight,
    value_weight,
    out_weight,
    mlp_in,
    mlp_in_bias,
    norm_gain,
    norm_bias,
    mlp_out,
    mlp_out_bias,
):
    own = descriptors[0]
    rows, width = own.shape
    hidden_width = mlp_in.shape[1]
    half = rows // 2
    images = lax.axis_size(("img", "pair"))
    place = lax.axis_index(RING).reshape(1)
    params = pltpu.CompilerParams(vmem_limit_bytes=40 << 20)

    own_weights = jnp.concatenate([qk_weight, value_weight], axis=1)
    swap = [(0, 1), (1, 0)]
    qk_other = lax.ppermute(qk_weight, "sub", swap)
    value_other = lax.ppermute(value_weight, "sub", swap)

    def carried(value, source):
        pairs = []
        for image in range(images):
            for sub in range(2):
                origin = source(image, sub)
                if origin is not None:
                    pairs.append((2 * origin[0] + origin[1], 2 * image + sub))
        return lax.ppermute(value, RING, pairs)

    def ahead(image, sub, step):
        partner = image + step if sub == 0 else image - step
        return partner if 0 <= partner < images else None

    def near(image, sub):
        return image % 2 == sub

    def within(image, sub):
        return (image ^ 1, image % 2) if near(image, sub) else None

    def by_two(image, sub):
        partner = ahead(image, sub, 2)
        return None if partner is None else (partner, sub)

    def outer(image, sub):
        partner = ahead(image, sub, 1)
        return None if near(image, sub) or partner is None else (partner, 1 - sub)

    def far_outer(image, sub):
        partner = ahead(image, sub, 3)
        if near(image, sub) or partner is None:
            return None
        return (partner ^ 1, (partner ^ 1) % 2)

    def far_inner(image, sub):
        if not near(image, sub) or ahead(image, sub, 3) is None:
            return None
        return (ahead(image, sub, 2), sub)

    one_inner = carried(own, within)
    two = carried(own, by_two)

    def called(kernel, args, out_shape, scratch, cost_estimate, scalars=1):
        return pl.pallas_call(
            kernel,
            in_specs=[SMEM] * scalars + [VMEM] * (len(args) - scalars),
            out_specs=[VMEM] * len(out_shape),
            out_shape=out_shape,
            scratch_shapes=scratch,
            compiler_params=params,
            cost_estimate=cost_estimate,
        )(*args)

    wk, wvt, queries, facts, own_half, vectors = called(
        functools.partial(prologue_kernel, images),
        [
            place, links.T, own, own_weights, qk_other, value_other,
            norm_gain.reshape(1, -1), norm_bias.reshape(1, -1), mlp_in_bias.reshape(1, -1),
            mlp_out_bias.reshape(1, -1),
        ],
        [
            shape((width, width), BF16),
            shape((width, width), BF16),
            shape((HEADS, rows, 128), BF16),
            shape((8, 128), F32),
            shape((half, width), BF16),
            shape((8, hidden_width), F32),
        ],
        [],
        cost(4 * rows * width * width, 4 << 20),
        scalars=2,
    )

    own_later, facts = lax.optimization_barrier((own, facts))
    one_outer = carried(own_later, outer)
    one_inner, facts = lax.optimization_barrier((one_inner, facts))
    three_outer = carried(one_inner, far_outer)
    three_inner = carried(one_inner, far_inner)

    projected = [
        shape((rows, width), BF16),
        shape((HEADS, width // HEADS + 16, rows), BF16),
    ]
    scratch = [pltpu.VMEM(x.shape, x.dtype) for x in projected]
    message_shape = [shape((width, rows), BF16)]
    work = cost(8 * rows * rows * width, 2 << 20, HEADS * rows * rows)
    half_work = cost(4 * rows * rows * width, 2 << 20, HEADS * rows * half)
    (message,) = called(
        functools.partial(partner_kernel, 2, False),
        [place, queries, facts, two, wk, wvt],
        message_shape,
        scratch,
        work,
    )
    one_outer, message = lax.optimization_barrier((one_outer, message))
    messages = [message]
    messages += called(
        functools.partial(partner_kernel, 1, True),
        [place, queries, facts, one_outer, one_inner, wk, wvt],
        message_shape,
        scratch,
        work,
    )
    three_outer, three_inner, messages = lax.optimization_barrier(
        (three_outer, three_inner, messages)
    )
    keys, values, send = called(
        functools.partial(last_kernel, 3),
        [place, queries, facts, three_outer, three_inner, wk, wvt, *messages],
        [*projected, shape((width, half), BF16)],
        [pltpu.VMEM((width, half), BF16)],
        half_work,
    )
    came = lax.ppermute(send, "sub", swap)
    (keep,) = called(
        functools.partial(own_kernel, 3),
        [place, queries, facts, keys, values, *messages],
        [shape((width, half), F32)],
        [pltpu.VMEM((width, half), BF16)],
        half_work,
    )
    came, keep = lax.optimization_barrier((came, keep))
    (result,) = called(
        tail_kernel,
        [keep, came, own_half, out_weight, mlp_in, vectors, mlp_out],
        [shape((half, width), BF16)],
        [],
        cost(4 * rows * width * width, 4 << 20),
        scalars=0,
    )
    return result[None]


def solution(mesh):
    placed = (
        P(("groups", "img", "pair"), None, None),
        P("groups", None),
        P(None, "sub"),
        P(None, "sub"),
        P(),
        P(),
        P(),
        P(),
        P(),
        P(),
        P(),
    )

    return jax.shard_map(
        on_device,
        mesh=mesh,
        in_specs=placed,
        out_specs=P(("groups", "img", "pair"), "sub", None),
        check_vma=False,
    )
```

```python
import functools
import math

import jax
import jax.numpy as jnp
from jax import lax
from jax.experimental import pallas as pl
from jax.experimental.pallas import tpu as pltpu
from jax.sharding import PartitionSpec as P


HEADS = 4
SPAN = 3
RING = ("img", "pair", "sub")
LEAST_SUM, LARGEST_SUM = 1e-20, 1e20
LARGEST_PRODUCT = 1e37
F32 = jnp.float32
BF16 = jnp.bfloat16
VMEM = pl.BlockSpec(memory_space=pltpu.VMEM)
SMEM = pl.BlockSpec(memory_space=pltpu.SMEM)


def dot(a, b, contract=(1, 0)):
    return lax.dot_general(
        a, b, (((contract[0],), (contract[1],)), ((), ())), preferred_element_type=F32
    )


def prologue_kernel(
    images, place_ref, links_ref, x_ref, own_ref, qk_other_ref, value_other_ref, gain_ref,
    shift_ref, bias_ref, out_bias_ref, wk_ref, wvt_ref, queries_ref, facts_ref, rows_ref, vectors_ref,
):
    rows, width = x_ref.shape
    local = width // 2
    sub = lax.rem(place_ref[0], 2)
    image = place_ref[0] // 2
    parts = []
    for i, other_ref in enumerate((qk_other_ref, value_other_ref)):
        own, other = own_ref[:, i * local : (i + 1) * local], other_ref[...]
        parts.append(jnp.where(sub == 0, own, other))
        parts.append(jnp.where(sub == 0, other, own))
    wk_ref[:, :local], wk_ref[:, local:] = parts[0], parts[1]
    wvt_ref[:local, :], wvt_ref[local:, :] = parts[2].T, parts[3].T
    keys = dot(x_ref[...], wk_ref[...]).astype(BF16)
    lane = lax.broadcasted_iota(jnp.int32, (rows, 128), 1)
    for head in range(HEADS):
        block, odd = head // 2 * 128, head % 2
        mine = (lane >= 64) if odd else (lane < 64)
        queries_ref[head] = jnp.where(mine, keys[:, block : block + 128], jnp.zeros((), BF16))
    for step in range(1, SPAN + 1):
        lower = image - sub * step
        inside = jnp.logical_and(lower >= 0, lower + step < images)
        entry = links_ref[step - 1, jnp.clip(lower, 0, images - 1)]
        linked = jnp.where(jnp.logical_and(inside, entry != 0), 1.0, 0.0)
        facts_ref[step : step + 1, :] = jnp.full((1, 128), linked, F32)
    half = rows // 2
    rows_ref[...] = x_ref[pl.ds(pl.multiple_of(sub * half, half), half), :]
    vectors_ref[0:1, :] = gain_ref[...]
    vectors_ref[1:2, :] = shift_ref[...]
    vectors_ref[2:3, :] = bias_ref[...]
    vectors_ref[3:4, :width] = out_bias_ref[...]


def project(x_ref, wk_ref, wvt_ref, keys_ref, values_ref):
    rows, width = keys_ref.shape
    head_width = width // HEADS
    tile = 256
    for r in range(0, rows, tile):
        x = x_ref[r : r + tile, :]
        keys_ref[r : r + tile, :] = dot(x, wk_ref[...]).astype(BF16)
        values = dot(wvt_ref[...], x, (1, 1)).astype(BF16)
        for head in range(HEADS):
            values_ref[head, :head_width, r : r + tile] = values[
                head * head_width : (head + 1) * head_width, :
            ]
            values_ref[head, head_width:, r : r + tile] = jnp.ones((16, tile), BF16)


def weigh(queries_ref, at, span, keys_ref, values_ref, done):
    rows, width = keys_ref.shape
    head_width = width // HEADS
    scale = math.log2(math.e) / math.sqrt(head_width)
    tile = 256
    queries_at = pl.ds(pl.multiple_of(at, span), span)
    sums = {}

    def finish(head, r, scores):
        weights = jnp.exp2(scores * scale).astype(BF16)
        product = dot(values_ref[head, :, r : r + tile], weights)
        sums[head] = product if r == 0 else sums[head] + product
        if r + tile == rows:
            done(head, sums[head])

    waiting = []
    for head in range(HEADS):
        queries = queries_ref[head, queries_at, :]
        lanes = slice(head // 2 * 128, head // 2 * 128 + 128)
        for r in range(0, rows, tile):
            waiting.append((head, r, dot(keys_ref[r : r + tile, lanes], queries, (1, 1))))
            if len(waiting) > 2:
                finish(*waiting.pop(0))
    for item in waiting:
        finish(*item)


def attend(queries_ref, at, span, pieces, message_ref, into, before_ref=None):
    width = pieces[0][0].shape[1]
    head_width = width // HEADS
    wrong = []

    def done(head, sums):
        if before_ref is not None:
            sums = sums + before_ref[head, :, pl.ds(pl.multiple_of(at, span), span)]
        total = sums[head_width : head_width + 1]
        message_ref[head * head_width : (head + 1) * head_width, into] = (
            sums[:head_width] * (1.0 / total)
        ).astype(BF16)
        top = jnp.max(jnp.abs(sums[:head_width]), axis=0, keepdims=True)
        fine = jnp.logical_and(total > LEAST_SUM, total < LARGEST_SUM)
        fine = jnp.logical_and(fine, top < LARGEST_PRODUCT)
        wrong.append(jnp.where(fine, 0.0, 1.0))

    weigh(queries_ref, at, span, *pieces[-1], done)

    @pl.when(jnp.max(sum(wrong)) > 0.0)
    def _():
        tile = 256

        def body(i, carry):
            head, part = i // (span // tile), lax.rem(i, span // tile)
            queries = queries_ref[head, pl.ds(pl.multiple_of(at + part * tile, tile), tile), :]
            lanes = pl.ds(pl.multiple_of(head // 2 * 128, 128), 128)
            scores = [dot(keys_ref[:, lanes], queries, (1, 1)) for keys_ref, _ in pieces]
            scores = jnp.concatenate(scores, axis=0) * (1.0 / math.sqrt(head_width))
            powers = jnp.exp(scores - jnp.max(scores, axis=0, keepdims=True))
            weights = (powers / jnp.sum(powers, axis=0, keepdims=True)).astype(BF16)
            product, start = 0.0, 0
            for keys_ref, values_ref in pieces:
                stop = start + keys_ref.shape[0]
                product = product + dot(values_ref[head, :head_width, :], weights[start:stop])
                start = stop
            head_rows = pl.ds(pl.multiple_of(head * head_width, head_width), head_width)
            columns = pl.ds(pl.multiple_of(into.start + part * tile, tile), tile)
            message_ref[head_rows, columns] = product.astype(BF16)
            return carry

        lax.fori_loop(0, HEADS * (span // tile), body, 0)


def is_linked(facts_ref, step):
    return jnp.max(facts_ref[step : step + 1, :]) > 0.0


def partner_kernel(
    step, queries_ref, facts_ref, x_ref, wk_ref, wvt_ref, message_ref, keys_ref, values_ref
):
    rows = keys_ref.shape[0]
    linked = is_linked(facts_ref, step)

    @pl.when(jnp.logical_not(linked))
    def _():
        message_ref[...] = jnp.zeros_like(message_ref)

    @pl.when(linked)
    def _():
        project(x_ref, wk_ref, wvt_ref, keys_ref, values_ref)
        wide = rows // 2

        def body(i, carry):
            at = pl.multiple_of(i * wide, wide)
            pieces = [(keys_ref, values_ref)]
            attend(queries_ref, at, wide, pieces, message_ref, pl.ds(at, wide))
            return carry

        lax.fori_loop(0, rows // wide, body, 0)


def first_half_kernel(
    step, queries_ref, facts_ref, x_ref, wk_ref, wvt_ref, keys_ref, values_ref, sums_ref
):
    @pl.when(is_linked(facts_ref, step))
    def _():
        project(x_ref, wk_ref, wvt_ref, keys_ref, values_ref)
        wide = keys_ref.shape[0]

        def body(i, carry):
            at = pl.multiple_of(i * wide, wide)

            def done(head, sums):
                sums_ref[head, :, pl.ds(at, wide)] = sums

            weigh(queries_ref, at, wide, keys_ref, values_ref, done)
            return carry

        lax.fori_loop(0, sums_ref.shape[2] // wide, body, 0)


def second_half_kernel(
    step, place_ref, queries_ref, facts_ref, x_ref, wk_ref, wvt_ref, keys_before_ref,
    values_before_ref, sums_ref, first_ref, second_ref, keys_ref, values_ref, send_ref, message_ref,
):
    half = message_ref.shape[1]
    at = pl.multiple_of((1 - lax.rem(place_ref[0], 2)) * half, half)
    here = pl.ds(at, half)
    linked = is_linked(facts_ref, step)

    @pl.when(jnp.logical_not(linked))
    def _():
        total = first_ref[:, here].astype(F32) + second_ref[:, here].astype(F32)
        send_ref[...] = total.astype(BF16)

    @pl.when(linked)
    def _():
        project(x_ref, wk_ref, wvt_ref, keys_ref, values_ref)
        pieces = [(keys_before_ref, values_before_ref), (keys_ref, values_ref)]
        attend(queries_ref, at, half, pieces, message_ref, pl.ds(0, half), sums_ref)
        total = first_ref[:, here].astype(F32) + second_ref[:, here].astype(F32)
        send_ref[...] = (total + message_ref[...].astype(F32)).astype(BF16)


def own_kernel(
    step, place_ref, queries_ref, facts_ref, keys_before_ref, values_before_ref, sums_ref, keys_ref,
    values_ref, first_ref, second_ref, keep_ref, message_ref,
):
    half = message_ref.shape[1]
    at = pl.multiple_of(lax.rem(place_ref[0], 2) * half, half)
    here = pl.ds(at, half)
    linked = is_linked(facts_ref, step)

    @pl.when(jnp.logical_not(linked))
    def _():
        keep_ref[...] = first_ref[:, here].astype(F32) + second_ref[:, here].astype(F32)

    @pl.when(linked)
    def _():
        pieces = [(keys_before_ref, values_before_ref), (keys_ref, values_ref)]
        attend(queries_ref, at, half, pieces, message_ref, pl.ds(0, half), sums_ref)
        total = first_ref[:, here].astype(F32) + second_ref[:, here].astype(F32)
        keep_ref[...] = total + message_ref[...].astype(F32)


def tail_kernel(
    keep_ref, came_ref, rows_ref, out_ref, mlp_ref, vectors_ref, mlp_out_ref, result_ref
):
    width = keep_ref.shape[0]
    own_rows = rows_ref[...]
    hidden = dot(own_rows, mlp_ref[:width, :]) + vectors_ref[2:3, :]
    summed = (keep_ref[...] + came_ref[...].astype(F32)).astype(BF16)
    projected = dot(summed, out_ref[...], (0, 0)).astype(BF16)
    hidden = hidden + dot(projected, mlp_ref[width:, :])
    centered = hidden - jnp.mean(hidden, axis=1, keepdims=True)
    variance = jnp.mean(centered * centered, axis=1, keepdims=True)
    normed = centered * lax.rsqrt(variance + 1e-05) * vectors_ref[0:1, :] + vectors_ref[1:2, :]
    activated = (0.5 * normed * (1.0 + lax.erf(normed * math.sqrt(0.5)))).astype(BF16)
    updated = dot(activated, mlp_out_ref[...]) + vectors_ref[3:4, :width]
    result_ref[...] = (updated + own_rows.astype(F32)).astype(BF16)


def shape(dims, dtype):
    return jax.ShapeDtypeStruct(dims, dtype)


def cost(flops, moved, exps=0):
    return pl.CostEstimate(flops=flops, bytes_accessed=moved, transcendentals=exps)


def on_device(
    descriptors,
    links,
    qk_weight,
    value_weight,
    out_weight,
    mlp_in,
    mlp_in_bias,
    norm_gain,
    norm_bias,
    mlp_out,
    mlp_out_bias,
):
    own = descriptors[0]
    rows, width = own.shape
    hidden_width = mlp_in.shape[1]
    half = rows // 2
    images = lax.axis_size(("img", "pair"))
    place = lax.axis_index(RING).reshape(1)
    params = pltpu.CompilerParams(vmem_limit_bytes=40 << 20)

    own_weights = jnp.concatenate([qk_weight, value_weight], axis=1)
    swap = [(0, 1), (1, 0)]
    qk_other = lax.ppermute(qk_weight, "sub", swap)
    value_other = lax.ppermute(value_weight, "sub", swap)

    def fetched(value, step):
        pairs = []
        for image in range(images):
            if image >= step:
                pairs.append((2 * image, 2 * (image - step)))
            if image + step < images:
                pairs.append((2 * image + 1, 2 * (image + step) + 1))
        return lax.ppermute(value, RING, pairs)

    three, two = fetched(own, 3), fetched(own, 2)
    own_later, qk_other = lax.optimization_barrier((own, qk_other))
    one_first = fetched(own_later[:half], 1)
    one_second = fetched(own_later[half:], 1)

    def called(kernel, args, out_shape, scratch, cost_estimate, scalars=1):
        return pl.pallas_call(
            kernel,
            in_specs=[SMEM] * scalars + [VMEM] * (len(args) - scalars),
            out_specs=[VMEM] * len(out_shape),
            out_shape=out_shape,
            scratch_shapes=scratch,
            compiler_params=params,
            cost_estimate=cost_estimate,
        )(*args)

    wk, wvt, queries, facts, own_half, vectors = called(
        functools.partial(prologue_kernel, images),
        [
            place, links.T, own, own_weights, qk_other, value_other,
            norm_gain.reshape(1, -1), norm_bias.reshape(1, -1), mlp_in_bias.reshape(1, -1),
            mlp_out_bias.reshape(1, -1),
        ],
        [
            shape((width, width), BF16),
            shape((width, width), BF16),
            shape((HEADS, rows, 128), BF16),
            shape((8, 128), F32),
            shape((half, width), BF16),
            shape((8, hidden_width), F32),
        ],
        [],
        cost(4 * rows * width * width, 4 << 20),
        scalars=2,
    )

    def projected(count):
        return [
            shape((count, width), BF16),
            shape((HEADS, width // HEADS + 16, count), BF16),
        ]

    scratch = [pltpu.VMEM(x.shape, x.dtype) for x in projected(rows)]
    message = [shape((width, rows), BF16)]
    work = cost(8 * rows * rows * width, 2 << 20, HEADS * rows * rows)
    half_work = cost(4 * rows * rows * width, 2 << 20, HEADS * rows * half)
    last_work = cost(2 * rows * rows * width, 2 << 20, HEADS * half * half)
    messages = []
    for step, partner in ((3, three), (2, two)):
        if messages:
            partner, messages = lax.optimization_barrier((partner, messages))
        messages += called(
            functools.partial(partner_kernel, step),
            [queries, facts, partner, wk, wvt],
            message,
            scratch,
            work,
            scalars=0,
        )
    one_first, messages = lax.optimization_barrier((one_first, messages))
    before = called(
        functools.partial(first_half_kernel, 1),
        [queries, facts, one_first, wk, wvt],
        [*projected(half), shape((HEADS, width // HEADS + 16, rows), F32)],
        [],
        half_work,
        scalars=0,
    )
    one_second, before = lax.optimization_barrier((one_second, before))
    keys, values, send = called(
        functools.partial(second_half_kernel, 1),
        [place, queries, facts, one_second, wk, wvt, *before, *messages],
        [*projected(half), shape((width, half), BF16)],
        [pltpu.VMEM((width, half), BF16)],
        last_work,
    )
    came = lax.ppermute(send, "sub", swap)
    (keep,) = called(
        functools.partial(own_kernel, 1),
        [place, queries, facts, *before, keys, values, *messages],
        [shape((width, half), F32)],
        [pltpu.VMEM((width, half), BF16)],
        last_work,
    )
    came, keep = lax.optimization_barrier((came, keep))
    (result,) = called(
        tail_kernel,
        [keep, came, own_half, out_weight, mlp_in, vectors, mlp_out],
        [shape((half, width), BF16)],
        [],
        cost(4 * rows * width * width, 4 << 20),
        scalars=0,
    )
    return result[None]


def solution(mesh):
    placed = (
        P(("groups", "img", "pair"), None, None),
        P("groups", None),
        P(None, "sub"),
        P(None, "sub"),
        P(),
        P(),
        P(),
        P(),
        P(),
        P(),
        P(),
    )

    return jax.shard_map(
        on_device,
        mesh=mesh,
        in_specs=placed,
        out_specs=P(("groups", "img", "pair"), "sub", None),
        check_vma=False,
    )
```

```python
import functools
import math

import jax
import jax.numpy as jnp
from jax import lax
from jax.experimental import pallas as pl
from jax.experimental.pallas import tpu as pltpu
from jax.sharding import PartitionSpec as P


HEADS = 4
SPAN = 3
RING = ("img", "pair", "sub")
LEAST_SUM, LARGEST_SUM = 1e-20, 1e20
LARGEST_PRODUCT = 1e37
F32 = jnp.float32
BF16 = jnp.bfloat16
VMEM = pl.BlockSpec(memory_space=pltpu.VMEM)
SMEM = pl.BlockSpec(memory_space=pltpu.SMEM)


def dot(a, b, contract=(1, 0)):
    return lax.dot_general(
        a, b, (((contract[0],), (contract[1],)), ((), ())), preferred_element_type=F32
    )


def prologue_kernel(
    images, place_ref, links_ref, x_ref, own_ref, qk_other_ref, value_other_ref, gain_ref,
    shift_ref, bias_ref, out_bias_ref, wk_ref, wvt_ref, queries_ref, facts_ref, rows_ref, vectors_ref,
):
    rows, width = x_ref.shape
    local = width // 2
    sub = lax.rem(place_ref[0], 2)
    image = place_ref[0] // 2
    parts = []
    for i, other_ref in enumerate((qk_other_ref, value_other_ref)):
        own, other = own_ref[:, i * local : (i + 1) * local], other_ref[...]
        parts.append(jnp.where(sub == 0, own, other))
        parts.append(jnp.where(sub == 0, other, own))
    wk_ref[:, :local], wk_ref[:, local:] = parts[0], parts[1]
    wvt_ref[:local, :], wvt_ref[local:, :] = parts[2].T, parts[3].T
    transposed = jnp.concatenate([parts[0].T, parts[1].T], axis=0)
    queries = dot(transposed, x_ref[...], (1, 1)).astype(BF16)
    head_width = width // HEADS
    for head in range(HEADS):
        mine, rest = (0, head_width) if head % 2 == 0 else (head_width, 0)
        queries_ref[head, mine : mine + head_width, :] = queries[
            head * head_width : (head + 1) * head_width, :
        ]
        queries_ref[head, rest : rest + head_width, :] = jnp.zeros((head_width, rows), BF16)
    for step in range(1, SPAN + 1):
        lower = image - sub * step
        inside = jnp.logical_and(lower >= 0, lower + step < images)
        entry = links_ref[step - 1, jnp.clip(lower, 0, images - 1)]
        linked = jnp.where(jnp.logical_and(inside, entry != 0), 1.0, 0.0)
        facts_ref[step : step + 1, :] = jnp.full((1, 128), linked, F32)
    half = rows // 2
    rows_ref[...] = x_ref[pl.ds(pl.multiple_of(sub * half, half), half), :]
    vectors_ref[0:1, :] = gain_ref[...]
    vectors_ref[1:2, :] = shift_ref[...]
    vectors_ref[2:3, :] = bias_ref[...]
    vectors_ref[3:4, :width] = out_bias_ref[...]


def project(x_ref, wk_ref, wvt_ref, keys_ref, values_ref):
    rows, width = keys_ref.shape
    head_width = width // HEADS
    tile = 256
    for r in range(0, rows, tile):
        x = x_ref[r : r + tile, :]
        keys_ref[r : r + tile, :] = dot(x, wk_ref[...]).astype(BF16)
        values = dot(wvt_ref[...], x, (1, 1)).astype(BF16)
        for head in range(HEADS):
            values_ref[head, :head_width, r : r + tile] = values[
                head * head_width : (head + 1) * head_width, :
            ]
            values_ref[head, head_width:, r : r + tile] = jnp.ones((16, tile), BF16)


def weigh(queries_ref, at, span, keys_ref, values_ref, done):
    rows, width = keys_ref.shape
    head_width = width // HEADS
    scale = math.log2(math.e) / math.sqrt(head_width)
    tile = 256
    queries_at = pl.ds(pl.multiple_of(at, span), span)
    sums = {}

    def finish(head, r, scores):
        weights = jnp.exp2(scores * scale).astype(BF16)
        product = dot(values_ref[head, :, r : r + tile], weights)
        sums[head] = product if r == 0 else sums[head] + product
        if r + tile == rows:
            done(head, sums[head])

    waiting = []
    for head in range(HEADS):
        queries = queries_ref[head, :, queries_at]
        lanes = slice(head // 2 * 128, head // 2 * 128 + 128)
        for r in range(0, rows, tile):
            waiting.append((head, r, dot(keys_ref[r : r + tile, lanes], queries)))
            if len(waiting) > 2:
                finish(*waiting.pop(0))
    for item in waiting:
        finish(*item)


def attend(queries_ref, at, span, pieces, message_ref, into, before_ref=None):
    width = pieces[0][0].shape[1]
    head_width = width // HEADS
    wrong = []

    def done(head, sums):
        if before_ref is not None:
            sums = sums + before_ref[head, :, pl.ds(pl.multiple_of(at, span), span)]
        total = sums[head_width : head_width + 1]
        message_ref[head * head_width : (head + 1) * head_width, into] = (
            sums[:head_width] * (1.0 / total)
        ).astype(BF16)
        top = jnp.max(jnp.abs(sums[:head_width]), axis=0, keepdims=True)
        fine = jnp.logical_and(total > LEAST_SUM, total < LARGEST_SUM)
        fine = jnp.logical_and(fine, top < LARGEST_PRODUCT)
        wrong.append(jnp.where(fine, 0.0, 1.0))

    weigh(queries_ref, at, span, *pieces[-1], done)

    @pl.when(jnp.max(sum(wrong)) > 0.0)
    def _():
        tile = 256

        def body(i, carry):
            head, part = i // (span // tile), lax.rem(i, span // tile)
            queries = queries_ref[head, :, pl.ds(pl.multiple_of(at + part * tile, tile), tile)]
            lanes = pl.ds(pl.multiple_of(head // 2 * 128, 128), 128)
            scores = [dot(keys_ref[:, lanes], queries) for keys_ref, _ in pieces]
            scores = jnp.concatenate(scores, axis=0) * (1.0 / math.sqrt(head_width))
            powers = jnp.exp(scores - jnp.max(scores, axis=0, keepdims=True))
            weights = (powers / jnp.sum(powers, axis=0, keepdims=True)).astype(BF16)
            product, start = 0.0, 0
            for keys_ref, values_ref in pieces:
                stop = start + keys_ref.shape[0]
                product = product + dot(values_ref[head, :head_width, :], weights[start:stop])
                start = stop
            head_rows = pl.ds(pl.multiple_of(head * head_width, head_width), head_width)
            columns = pl.ds(pl.multiple_of(into.start + part * tile, tile), tile)
            message_ref[head_rows, columns] = product.astype(BF16)
            return carry

        lax.fori_loop(0, HEADS * (span // tile), body, 0)


def is_linked(facts_ref, step):
    return jnp.max(facts_ref[step : step + 1, :]) > 0.0


def partner_kernel(
    step, queries_ref, facts_ref, x_ref, wk_ref, wvt_ref, message_ref, keys_ref, values_ref
):
    rows = keys_ref.shape[0]
    linked = is_linked(facts_ref, step)

    @pl.when(jnp.logical_not(linked))
    def _():
        message_ref[...] = jnp.zeros_like(message_ref)

    @pl.when(linked)
    def _():
        project(x_ref, wk_ref, wvt_ref, keys_ref, values_ref)
        wide = rows // 2

        def body(i, carry):
            at = pl.multiple_of(i * wide, wide)
            pieces = [(keys_ref, values_ref)]
            attend(queries_ref, at, wide, pieces, message_ref, pl.ds(at, wide))
            return carry

        lax.fori_loop(0, rows // wide, body, 0)


def first_half_kernel(
    step, queries_ref, facts_ref, x_ref, wk_ref, wvt_ref, keys_ref, values_ref, sums_ref
):
    @pl.when(is_linked(facts_ref, step))
    def _():
        project(x_ref, wk_ref, wvt_ref, keys_ref, values_ref)
        wide = keys_ref.shape[0]

        def body(i, carry):
            at = pl.multiple_of(i * wide, wide)

            def done(head, sums):
                sums_ref[head, :, pl.ds(at, wide)] = sums

            weigh(queries_ref, at, wide, keys_ref, values_ref, done)
            return carry

        lax.fori_loop(0, sums_ref.shape[2] // wide, body, 0)


def second_half_kernel(
    step, place_ref, queries_ref, facts_ref, x_ref, wk_ref, wvt_ref, keys_before_ref,
    values_before_ref, sums_ref, first_ref, second_ref, keys_ref, values_ref, send_ref, message_ref,
):
    half = message_ref.shape[1]
    at = pl.multiple_of((1 - lax.rem(place_ref[0], 2)) * half, half)
    here = pl.ds(at, half)
    linked = is_linked(facts_ref, step)

    @pl.when(jnp.logical_not(linked))
    def _():
        total = first_ref[:, here].astype(F32) + second_ref[:, here].astype(F32)
        send_ref[...] = total.astype(BF16)

    @pl.when(linked)
    def _():
        project(x_ref, wk_ref, wvt_ref, keys_ref, values_ref)
        pieces = [(keys_before_ref, values_before_ref), (keys_ref, values_ref)]
        attend(queries_ref, at, half, pieces, message_ref, pl.ds(0, half), sums_ref)
        total = first_ref[:, here].astype(F32) + second_ref[:, here].astype(F32)
        send_ref[...] = (total + message_ref[...].astype(F32)).astype(BF16)


def own_kernel(
    step, place_ref, queries_ref, facts_ref, keys_before_ref, values_before_ref, sums_ref, keys_ref,
    values_ref, first_ref, second_ref, keep_ref, message_ref,
):
    half = message_ref.shape[1]
    at = pl.multiple_of(lax.rem(place_ref[0], 2) * half, half)
    here = pl.ds(at, half)
    linked = is_linked(facts_ref, step)

    @pl.when(jnp.logical_not(linked))
    def _():
        keep_ref[...] = first_ref[:, here].astype(F32) + second_ref[:, here].astype(F32)

    @pl.when(linked)
    def _():
        pieces = [(keys_before_ref, values_before_ref), (keys_ref, values_ref)]
        attend(queries_ref, at, half, pieces, message_ref, pl.ds(0, half), sums_ref)
        total = first_ref[:, here].astype(F32) + second_ref[:, here].astype(F32)
        keep_ref[...] = total + message_ref[...].astype(F32)


def tail_kernel(
    keep_ref, came_ref, rows_ref, out_ref, mlp_ref, vectors_ref, mlp_out_ref, result_ref
):
    width = keep_ref.shape[0]
    own_rows = rows_ref[...]
    hidden = dot(own_rows, mlp_ref[:width, :]) + vectors_ref[2:3, :]
    summed = (keep_ref[...] + came_ref[...].astype(F32)).astype(BF16)
    projected = dot(summed, out_ref[...], (0, 0)).astype(BF16)
    hidden = hidden + dot(projected, mlp_ref[width:, :])
    centered = hidden - jnp.mean(hidden, axis=1, keepdims=True)
    variance = jnp.mean(centered * centered, axis=1, keepdims=True)
    normed = centered * lax.rsqrt(variance + 1e-05) * vectors_ref[0:1, :] + vectors_ref[1:2, :]
    activated = (0.5 * normed * (1.0 + lax.erf(normed * math.sqrt(0.5)))).astype(BF16)
    updated = dot(activated, mlp_out_ref[...]) + vectors_ref[3:4, :width]
    result_ref[...] = (updated + own_rows.astype(F32)).astype(BF16)


def shape(dims, dtype):
    return jax.ShapeDtypeStruct(dims, dtype)


def cost(flops, moved, exps=0):
    return pl.CostEstimate(flops=flops, bytes_accessed=moved, transcendentals=exps)


def on_device(
    descriptors,
    links,
    qk_weight,
    value_weight,
    out_weight,
    mlp_in,
    mlp_in_bias,
    norm_gain,
    norm_bias,
    mlp_out,
    mlp_out_bias,
):
    own = descriptors[0]
    rows, width = own.shape
    hidden_width = mlp_in.shape[1]
    half = rows // 2
    images = lax.axis_size(("img", "pair"))
    place = lax.axis_index(RING).reshape(1)
    params = pltpu.CompilerParams(vmem_limit_bytes=40 << 20)

    own_weights = jnp.concatenate([qk_weight, value_weight], axis=1)
    swap = [(0, 1), (1, 0)]
    qk_other = lax.ppermute(qk_weight, "sub", swap)
    value_other = lax.ppermute(value_weight, "sub", swap)

    def fetched(value, step):
        pairs = []
        for image in range(images):
            if image >= step:
                pairs.append((2 * image, 2 * (image - step)))
            if image + step < images:
                pairs.append((2 * image + 1, 2 * (image + step) + 1))
        return lax.ppermute(value, RING, pairs)

    three, two = fetched(own, 3), fetched(own, 2)
    own_later, qk_other = lax.optimization_barrier((own, qk_other))
    one_first = fetched(own_later[:half], 1)
    one_second = fetched(own_later[half:], 1)

    def called(kernel, args, out_shape, scratch, cost_estimate, scalars=1):
        return pl.pallas_call(
            kernel,
            in_specs=[SMEM] * scalars + [VMEM] * (len(args) - scalars),
            out_specs=[VMEM] * len(out_shape),
            out_shape=out_shape,
            scratch_shapes=scratch,
            compiler_params=params,
            cost_estimate=cost_estimate,
        )(*args)

    wk, wvt, queries, facts, own_half, vectors = called(
        functools.partial(prologue_kernel, images),
        [
            place, links.T, own, own_weights, qk_other, value_other,
            norm_gain.reshape(1, -1), norm_bias.reshape(1, -1), mlp_in_bias.reshape(1, -1),
            mlp_out_bias.reshape(1, -1),
        ],
        [
            shape((width, width), BF16),
            shape((width, width), BF16),
            shape((HEADS, 128, rows), BF16),
            shape((8, 128), F32),
            shape((half, width), BF16),
            shape((8, hidden_width), F32),
        ],
        [],
        cost(4 * rows * width * width, 4 << 20),
        scalars=2,
    )

    def projected(count):
        return [
            shape((count, width), BF16),
            shape((HEADS, width // HEADS + 16, count), BF16),
        ]

    scratch = [pltpu.VMEM(x.shape, x.dtype) for x in projected(rows)]
    message = [shape((width, rows), BF16)]
    work = cost(8 * rows * rows * width, 2 << 20, HEADS * rows * rows)
    half_work = cost(4 * rows * rows * width, 2 << 20, HEADS * rows * half)
    last_work = cost(2 * rows * rows * width, 2 << 20, HEADS * half * half)
    messages = []
    for step, partner in ((3, three), (2, two)):
        if messages:
            partner, messages = lax.optimization_barrier((partner, messages))
        messages += called(
            functools.partial(partner_kernel, step),
            [queries, facts, partner, wk, wvt],
            message,
            scratch,
            work,
            scalars=0,
        )
    one_first, messages = lax.optimization_barrier((one_first, messages))
    before = called(
        functools.partial(first_half_kernel, 1),
        [queries, facts, one_first, wk, wvt],
        [*projected(half), shape((HEADS, width // HEADS + 16, rows), F32)],
        [],
        half_work,
        scalars=0,
    )
    one_second, before = lax.optimization_barrier((one_second, before))
    keys, values, send = called(
        functools.partial(second_half_kernel, 1),
        [place, queries, facts, one_second, wk, wvt, *before, *messages],
        [*projected(half), shape((width, half), BF16)],
        [pltpu.VMEM((width, half), BF16)],
        last_work,
    )
    came = lax.ppermute(send, "sub", swap)
    (keep,) = called(
        functools.partial(own_kernel, 1),
        [place, queries, facts, *before, keys, values, *messages],
        [shape((width, half), F32)],
        [pltpu.VMEM((width, half), BF16)],
        last_work,
    )
    came, keep = lax.optimization_barrier((came, keep))
    (result,) = called(
        tail_kernel,
        [keep, came, own_half, out_weight, mlp_in, vectors, mlp_out],
        [shape((half, width), BF16)],
        [],
        cost(4 * rows * width * width, 4 << 20),
        scalars=0,
    )
    return result[None]


def solution(mesh):
    placed = (
        P(("groups", "img", "pair"), None, None),
        P("groups", None),
        P(None, "sub"),
        P(None, "sub"),
        P(),
        P(),
        P(),
        P(),
        P(),
        P(),
        P(),
    )

    return jax.shard_map(
        on_device,
        mesh=mesh,
        in_specs=placed,
        out_specs=P(("groups", "img", "pair"), "sub", None),
        check_vma=False,
    )
```

```python
import functools
import math

import jax
import jax.numpy as jnp
from jax import lax
from jax.experimental import pallas as pl
from jax.experimental.pallas import tpu as pltpu
from jax.sharding import PartitionSpec as P


HEADS = 4
SPAN = 3
RING = ("img", "pair", "sub")
LEAST_SUM, LARGEST_SUM = 1e-20, 1e20
LARGEST_PRODUCT = 1e37
F32 = jnp.float32
BF16 = jnp.bfloat16
VMEM = pl.BlockSpec(memory_space=pltpu.VMEM)
SMEM = pl.BlockSpec(memory_space=pltpu.SMEM)


def dot(a, b, contract=(1, 0)):
    return lax.dot_general(
        a, b, (((contract[0],), (contract[1],)), ((), ())), preferred_element_type=F32
    )


def prologue_kernel(
    images, place_ref, links_ref, x_ref, qk_ref, value_ref, qk_other_ref, value_other_ref, gain_ref,
    shift_ref, bias_ref, out_bias_ref, wk_ref, wvt_ref, queries_ref, facts_ref, rows_ref, vectors_ref,
):
    rows, width = x_ref.shape
    local = width // 2
    sub = lax.rem(place_ref[0], 2)
    image = place_ref[0] // 2
    parts = []
    for own_ref, other_ref in ((qk_ref, qk_other_ref), (value_ref, value_other_ref)):
        own, other = own_ref[...], other_ref[...]
        parts.append(jnp.where(sub == 0, own, other))
        parts.append(jnp.where(sub == 0, other, own))
    wk_ref[:, :local], wk_ref[:, local:] = parts[0], parts[1]
    wvt_ref[:local, :], wvt_ref[local:, :] = parts[2].T, parts[3].T
    transposed = jnp.concatenate([parts[0].T, parts[1].T], axis=0)
    queries = dot(transposed, x_ref[...], (1, 1)).astype(BF16)
    head_width = width // HEADS
    for head in range(HEADS):
        mine, rest = (0, head_width) if head % 2 == 0 else (head_width, 0)
        queries_ref[head, mine : mine + head_width, :] = queries[
            head * head_width : (head + 1) * head_width, :
        ]
        queries_ref[head, rest : rest + head_width, :] = jnp.zeros((head_width, rows), BF16)
    for step in range(1, SPAN + 1):
        lower = image - sub * step
        inside = jnp.logical_and(lower >= 0, lower + step < images)
        entry = links_ref[step - 1, jnp.clip(lower, 0, images - 1)]
        linked = jnp.where(jnp.logical_and(inside, entry != 0), 1.0, 0.0)
        facts_ref[step : step + 1, :] = jnp.full((1, 128), linked, F32)
    half = rows // 2
    rows_ref[...] = x_ref[pl.ds(pl.multiple_of(sub * half, half), half), :]
    vectors_ref[0:1, :] = gain_ref[...]
    vectors_ref[1:2, :] = shift_ref[...]
    vectors_ref[2:3, :] = bias_ref[...]
    vectors_ref[3:4, :width] = out_bias_ref[...]


def project(x_ref, wk_ref, wvt_ref, keys_ref, values_ref):
    rows, width = keys_ref.shape
    head_width = width // HEADS
    tile = 256
    for r in range(0, rows, tile):
        x = x_ref[r : r + tile, :]
        keys_ref[r : r + tile, :] = dot(x, wk_ref[...]).astype(BF16)
        values = dot(wvt_ref[...], x, (1, 1)).astype(BF16)
        for head in range(HEADS):
            values_ref[head, :head_width, r : r + tile] = values[
                head * head_width : (head + 1) * head_width, :
            ]
            values_ref[head, head_width:, r : r + tile] = jnp.ones((16, tile), BF16)


def attend(queries_ref, at, span, keys_ref, values_ref, message_ref, into):
    rows, width = keys_ref.shape
    head_width = width // HEADS
    scale = 1.0 / math.sqrt(head_width)
    tile = 256
    queries_at = pl.ds(pl.multiple_of(at, span), span)
    totals = {}
    wrong = []

    def finish(head, r, scores):
        weights = jnp.exp2(scores * (scale * math.log2(math.e))).astype(BF16)
        product = dot(values_ref[head, :, r : r + tile], weights)
        total = product if r == 0 else totals[head] + product
        totals[head] = total
        if r + tile == rows:
            sums = total[head_width : head_width + 1]
            message_ref[head * head_width : (head + 1) * head_width, into] = (
                total[:head_width] * (1.0 / sums)
            ).astype(BF16)
            top = jnp.max(jnp.abs(total[:head_width]), axis=0, keepdims=True)
            fine = jnp.logical_and(sums > LEAST_SUM, sums < LARGEST_SUM)
            fine = jnp.logical_and(fine, top < LARGEST_PRODUCT)
            wrong.append(jnp.where(fine, 0.0, 1.0))

    waiting = []
    for head in range(HEADS):
        queries = queries_ref[head, :, queries_at]
        lanes = slice(head // 2 * 128, head // 2 * 128 + 128)
        for r in range(0, rows, tile):
            waiting.append((head, r, dot(keys_ref[r : r + tile, lanes], queries)))
            if len(waiting) > 2:
                finish(*waiting.pop(0))
    for item in waiting:
        finish(*item)

    @pl.when(jnp.max(sum(wrong)) > 0.0)
    def _():
        def body(i, carry):
            head, part = i // (span // tile), lax.rem(i, span // tile)
            part_at = pl.ds(pl.multiple_of(at + part * tile, tile), tile)
            lanes = pl.ds(pl.multiple_of(head // 2 * 128, 128), 128)
            scores = dot(keys_ref[:, lanes], queries_ref[head, :, part_at]) * scale
            powers = jnp.exp(scores - jnp.max(scores, axis=0, keepdims=True))
            weights = powers / jnp.sum(powers, axis=0, keepdims=True)
            product = dot(values_ref[head, :head_width, :], weights.astype(BF16))
            head_rows = pl.ds(pl.multiple_of(head * head_width, head_width), head_width)
            columns = pl.ds(pl.multiple_of(into.start + part * tile, tile), tile)
            message_ref[head_rows, columns] = product.astype(BF16)
            return carry

        lax.fori_loop(0, HEADS * (span // tile), body, 0)


def partner_kernel(
    step, queries_ref, facts_ref, x_ref, wk_ref, wvt_ref, message_ref, keys_ref, values_ref
):
    rows, _ = keys_ref.shape
    linked = jnp.max(facts_ref[step : step + 1, :]) > 0.0

    @pl.when(jnp.logical_not(linked))
    def _():
        message_ref[...] = jnp.zeros_like(message_ref)

    @pl.when(linked)
    def _():
        project(x_ref, wk_ref, wvt_ref, keys_ref, values_ref)
        wide = rows // 2

        def body(i, carry):
            at = pl.multiple_of(i * wide, wide)
            attend(queries_ref, at, wide, keys_ref, values_ref, message_ref, pl.ds(at, wide))
            return carry

        lax.fori_loop(0, rows // wide, body, 0)


def last_kernel(
    step, place_ref, queries_ref, facts_ref, x_ref, wk_ref, wvt_ref, first_ref, second_ref,
    keys_ref, values_ref, send_ref, message_ref,
):
    half = message_ref.shape[1]
    place = place_ref[0]
    at = pl.multiple_of((1 - lax.rem(place, 2)) * half, half)
    here = pl.ds(at, half)
    linked = jnp.max(facts_ref[step : step + 1, :]) > 0.0
    total = first_ref[:, here].astype(F32) + second_ref[:, here].astype(F32)

    @pl.when(jnp.logical_not(linked))
    def _():
        send_ref[...] = total.astype(BF16)

    @pl.when(linked)
    def _():
        project(x_ref, wk_ref, wvt_ref, keys_ref, values_ref)
        attend(queries_ref, at, half, keys_ref, values_ref, message_ref, pl.ds(0, half))
        total = first_ref[:, here].astype(F32) + second_ref[:, here].astype(F32)
        send_ref[...] = (total + message_ref[...].astype(F32)).astype(BF16)


def own_kernel(
    step, place_ref, queries_ref, facts_ref, keys_ref, values_ref, first_ref, second_ref, keep_ref,
    message_ref,
):
    half = message_ref.shape[1]
    at = pl.multiple_of(lax.rem(place_ref[0], 2) * half, half)
    here = pl.ds(at, half)
    linked = jnp.max(facts_ref[step : step + 1, :]) > 0.0

    @pl.when(jnp.logical_not(linked))
    def _():
        keep_ref[...] = first_ref[:, here].astype(F32) + second_ref[:, here].astype(F32)

    @pl.when(linked)
    def _():
        attend(queries_ref, at, half, keys_ref, values_ref, message_ref, pl.ds(0, half))
        total = first_ref[:, here].astype(F32) + second_ref[:, here].astype(F32)
        keep_ref[...] = total + message_ref[...].astype(F32)


def tail_kernel(
    keep_ref, came_ref, rows_ref, out_ref, mlp_ref, vectors_ref, mlp_out_ref, result_ref
):
    width = keep_ref.shape[0]
    own_rows = rows_ref[...]
    hidden = dot(own_rows, mlp_ref[:width, :]) + vectors_ref[2:3, :]
    summed = (keep_ref[...] + came_ref[...].astype(F32)).astype(BF16)
    projected = dot(summed, out_ref[...], (0, 0)).astype(BF16)
    hidden = hidden + dot(projected, mlp_ref[width:, :])
    centered = hidden - jnp.mean(hidden, axis=1, keepdims=True)
    variance = jnp.mean(centered * centered, axis=1, keepdims=True)
    normed = centered * lax.rsqrt(variance + 1e-05) * vectors_ref[0:1, :] + vectors_ref[1:2, :]
    activated = (0.5 * normed * (1.0 + lax.erf(normed * math.sqrt(0.5)))).astype(BF16)
    updated = dot(activated, mlp_out_ref[...]) + vectors_ref[3:4, :width]
    result_ref[...] = (updated + own_rows.astype(F32)).astype(BF16)


def shape(dims, dtype):
    return jax.ShapeDtypeStruct(dims, dtype)


def cost(flops, moved, exps=0):
    return pl.CostEstimate(flops=flops, bytes_accessed=moved, transcendentals=exps)


def on_device(
    descriptors,
    links,
    qk_weight,
    value_weight,
    out_weight,
    mlp_in,
    mlp_in_bias,
    norm_gain,
    norm_bias,
    mlp_out,
    mlp_out_bias,
):
    own = descriptors[0]
    rows, width = own.shape
    hidden_width = mlp_in.shape[1]
    half = rows // 2
    images = lax.axis_size(("img", "pair"))
    place = lax.axis_index(RING).reshape(1)
    params = pltpu.CompilerParams(vmem_limit_bytes=40 << 20)

    swap = [(0, 1), (1, 0)]
    qk_other = lax.ppermute(qk_weight, "sub", swap)
    value_other = lax.ppermute(value_weight, "sub", swap)

    def fetched(step):
        pairs = []
        for image in range(images):
            if image >= step:
                pairs.append((2 * image, 2 * (image - step)))
            if image + step < images:
                pairs.append((2 * image + 1, 2 * (image + step) + 1))
        return lax.ppermute(own, RING, pairs)

    three, two, one = (fetched(step) for step in (3, 2, 1))

    def called(kernel, args, out_shape, scratch, cost_estimate, scalars=1):
        return pl.pallas_call(
            kernel,
            in_specs=[SMEM] * scalars + [VMEM] * (len(args) - scalars),
            out_specs=[VMEM] * len(out_shape),
            out_shape=out_shape,
            scratch_shapes=scratch,
            compiler_params=params,
            cost_estimate=cost_estimate,
        )(*args)

    wk, wvt, queries, facts, own_half, vectors = called(
        functools.partial(prologue_kernel, images),
        [
            place, links.T, own, qk_weight, value_weight, qk_other, value_other,
            norm_gain.reshape(1, -1), norm_bias.reshape(1, -1), mlp_in_bias.reshape(1, -1),
            mlp_out_bias.reshape(1, -1),
        ],
        [
            shape((width, width), BF16),
            shape((width, width), BF16),
            shape((HEADS, 128, rows), BF16),
            shape((8, 128), F32),
            shape((half, width), BF16),
            shape((8, hidden_width), F32),
        ],
        [],
        cost(4 * rows * width * width, 4 << 20),
        scalars=2,
    )

    projected = [
        shape((rows, width), BF16),
        shape((HEADS, width // HEADS + 16, rows), BF16),
    ]
    scratch = [pltpu.VMEM(x.shape, x.dtype) for x in projected]
    message = [shape((width, rows), BF16)]
    work = cost(8 * rows * rows * width, 2 << 20, HEADS * rows * rows)
    half_work = cost(4 * rows * rows * width, 2 << 20, HEADS * rows * half)
    messages = []
    for step, partner in ((3, three), (2, two)):
        if messages:
            partner, messages = lax.optimization_barrier((partner, messages))
        messages += called(
            functools.partial(partner_kernel, step),
            [queries, facts, partner, wk, wvt],
            message,
            scratch,
            work,
            scalars=0,
        )
    one, messages = lax.optimization_barrier((one, messages))
    keys, values, send = called(
        functools.partial(last_kernel, 1),
        [place, queries, facts, one, wk, wvt, *messages],
        [*projected, shape((width, half), BF16)],
        [pltpu.VMEM((width, half), BF16)],
        half_work,
    )
    came = lax.ppermute(send, "sub", swap)
    (keep,) = called(
        functools.partial(own_kernel, 1),
        [place, queries, facts, keys, values, *messages],
        [shape((width, half), F32)],
        [pltpu.VMEM((width, half), BF16)],
        half_work,
    )
    came, keep = lax.optimization_barrier((came, keep))
    (result,) = called(
        tail_kernel,
        [keep, came, own_half, out_weight, mlp_in, vectors, mlp_out],
        [shape((half, width), BF16)],
        [],
        cost(4 * rows * width * width, 4 << 20),
        scalars=0,
    )
    return result[None]


def solution(mesh):
    placed = (
        P(("groups", "img", "pair"), None, None),
        P("groups", None),
        P(None, "sub"),
        P(None, "sub"),
        P(),
        P(),
        P(),
        P(),
        P(),
        P(),
        P(),
    )

    return jax.shard_map(
        on_device,
        mesh=mesh,
        in_specs=placed,
        out_specs=P(("groups", "img", "pair"), "sub", None),
        check_vma=False,
    )
```

```python
import functools
import math

import jax
import jax.numpy as jnp
from jax import lax
from jax.experimental import pallas as pl
from jax.experimental.pallas import tpu as pltpu
from jax.sharding import PartitionSpec as P


HEADS = 4
SPAN = 3
RING = ("img", "pair", "sub")
LEAST_SUM, LARGEST_SUM = 1e-20, 1e20
LARGEST_PRODUCT = 1e37
F32 = jnp.float32
BF16 = jnp.bfloat16
VMEM = pl.BlockSpec(memory_space=pltpu.VMEM)
SMEM = pl.BlockSpec(memory_space=pltpu.SMEM)


def dot(a, b, contract=(1, 0)):
    return lax.dot_general(
        a, b, (((contract[0],), (contract[1],)), ((), ())), preferred_element_type=F32
    )


def prologue_kernel(
    images, place_ref, links_ref, x_ref, own_ref, qk_other_ref, value_other_ref, gain_ref,
    shift_ref, bias_ref, out_bias_ref, wk_ref, wvt_ref, queries_ref, facts_ref, rows_ref, vectors_ref,
):
    rows, width = x_ref.shape
    local = width // 2
    sub = lax.rem(place_ref[0], 2)
    image = place_ref[0] // 2
    parts = []
    for i, other_ref in enumerate((qk_other_ref, value_other_ref)):
        own, other = own_ref[:, i * local : (i + 1) * local], other_ref[...]
        parts.append(jnp.where(sub == 0, own, other))
        parts.append(jnp.where(sub == 0, other, own))
    wk_ref[:, :local], wk_ref[:, local:] = parts[0], parts[1]
    wvt_ref[:local, :], wvt_ref[local:, :] = parts[2].T, parts[3].T
    transposed = jnp.concatenate([parts[0].T, parts[1].T], axis=0)
    queries = dot(transposed, x_ref[...], (1, 1)).astype(BF16)
    head_width = width // HEADS
    for head in range(HEADS):
        mine, rest = (0, head_width) if head % 2 == 0 else (head_width, 0)
        queries_ref[head, mine : mine + head_width, :] = queries[
            head * head_width : (head + 1) * head_width, :
        ]
        queries_ref[head, rest : rest + head_width, :] = jnp.zeros((head_width, rows), BF16)
    for step in range(1, SPAN + 1):
        lower = image - sub * step
        inside = jnp.logical_and(lower >= 0, lower + step < images)
        entry = links_ref[step - 1, jnp.clip(lower, 0, images - 1)]
        linked = jnp.where(jnp.logical_and(inside, entry != 0), 1.0, 0.0)
        facts_ref[step : step + 1, :] = jnp.full((1, 128), linked, F32)
    half = rows // 2
    rows_ref[...] = x_ref[pl.ds(pl.multiple_of(sub * half, half), half), :]
    vectors_ref[0:1, :] = gain_ref[...]
    vectors_ref[1:2, :] = shift_ref[...]
    vectors_ref[2:3, :] = bias_ref[...]
    vectors_ref[3:4, :width] = out_bias_ref[...]


def project(x_ref, other_ref, take_other, wk_ref, wvt_ref, keys_ref, values_ref):
    rows, width = keys_ref.shape
    head_width = width // HEADS
    tile = 256
    for r in range(0, rows, tile):
        x = x_ref[r : r + tile, :]
        if other_ref is not None:
            x = jnp.where(take_other, other_ref[r : r + tile, :], x)
        keys_ref[r : r + tile, :] = dot(x, wk_ref[...]).astype(BF16)
        values = dot(wvt_ref[...], x, (1, 1)).astype(BF16)
        for head in range(HEADS):
            values_ref[head, :head_width, r : r + tile] = values[
                head * head_width : (head + 1) * head_width, :
            ]
            values_ref[head, head_width:, r : r + tile] = jnp.ones((16, tile), BF16)


def attend(queries_ref, at, span, keys_ref, values_ref, message_ref, into):
    rows, width = keys_ref.shape
    head_width = width // HEADS
    scale = 1.0 / math.sqrt(head_width)
    tile = 256
    queries_at = pl.ds(pl.multiple_of(at, span), span)
    totals = {}
    wrong = []

    def finish(head, r, scores):
        weights = jnp.exp2(scores * (scale * math.log2(math.e))).astype(BF16)
        product = dot(values_ref[head, :, r : r + tile], weights)
        total = product if r == 0 else totals[head] + product
        totals[head] = total
        if r + tile == rows:
            sums = total[head_width : head_width + 1]
            message_ref[head * head_width : (head + 1) * head_width, into] = (
                total[:head_width] * (1.0 / sums)
            ).astype(BF16)
            top = jnp.max(jnp.abs(total[:head_width]), axis=0, keepdims=True)
            fine = jnp.logical_and(sums > LEAST_SUM, sums < LARGEST_SUM)
            fine = jnp.logical_and(fine, top < LARGEST_PRODUCT)
            wrong.append(jnp.where(fine, 0.0, 1.0))

    waiting = []
    for head in range(HEADS):
        queries = queries_ref[head, :, queries_at]
        lanes = slice(head // 2 * 128, head // 2 * 128 + 128)
        for r in range(0, rows, tile):
            waiting.append((head, r, dot(keys_ref[r : r + tile, lanes], queries)))
            if len(waiting) > 2:
                finish(*waiting.pop(0))
    for item in waiting:
        finish(*item)

    @pl.when(jnp.max(sum(wrong)) > 0.0)
    def _():
        def body(i, carry):
            head, part = i // (span // tile), lax.rem(i, span // tile)
            part_at = pl.ds(pl.multiple_of(at + part * tile, tile), tile)
            lanes = pl.ds(pl.multiple_of(head // 2 * 128, 128), 128)
            scores = dot(keys_ref[:, lanes], queries_ref[head, :, part_at]) * scale
            powers = jnp.exp(scores - jnp.max(scores, axis=0, keepdims=True))
            weights = powers / jnp.sum(powers, axis=0, keepdims=True)
            product = dot(values_ref[head, :head_width, :], weights.astype(BF16))
            head_rows = pl.ds(pl.multiple_of(head * head_width, head_width), head_width)
            columns = pl.ds(pl.multiple_of(into.start + part * tile, tile), tile)
            message_ref[head_rows, columns] = product.astype(BF16)
            return carry

        lax.fori_loop(0, HEADS * (span // tile), body, 0)


def near_first(place):
    return lax.rem(place // 2, 2) == lax.rem(place, 2)


def is_linked(facts_ref, steps, place):
    near, far = (jnp.max(facts_ref[step : step + 1, :]) for step in steps)
    return jnp.where(near_first(place), near, far) > 0.0


def partner_kernel(steps, two, place_ref, queries_ref, facts_ref, x_ref, *refs):
    other_ref, *refs = refs if two else (None, *refs)
    wk_ref, wvt_ref, message_ref, keys_ref, values_ref = refs
    rows, _ = keys_ref.shape
    linked = is_linked(facts_ref, steps, place_ref[0])

    @pl.when(jnp.logical_not(linked))
    def _():
        message_ref[...] = jnp.zeros_like(message_ref)

    @pl.when(linked)
    def _():
        take = near_first(place_ref[0])
        project(x_ref, other_ref, take, wk_ref, wvt_ref, keys_ref, values_ref)
        wide = rows // 2

        def body(i, carry):
            at = pl.multiple_of(i * wide, wide)
            attend(queries_ref, at, wide, keys_ref, values_ref, message_ref, pl.ds(at, wide))
            return carry

        lax.fori_loop(0, rows // wide, body, 0)


def last_kernel(
    steps, place_ref, queries_ref, facts_ref, x_ref, other_ref, wk_ref, wvt_ref, first_ref,
    second_ref, keys_ref, values_ref, send_ref, message_ref,
):
    half = message_ref.shape[1]
    place = place_ref[0]
    at = pl.multiple_of((1 - lax.rem(place, 2)) * half, half)
    here = pl.ds(at, half)
    linked = is_linked(facts_ref, steps, place_ref[0])
    total = first_ref[:, here].astype(F32) + second_ref[:, here].astype(F32)

    @pl.when(jnp.logical_not(linked))
    def _():
        send_ref[...] = total.astype(BF16)

    @pl.when(linked)
    def _():
        project(x_ref, other_ref, near_first(place), wk_ref, wvt_ref, keys_ref, values_ref)
        attend(queries_ref, at, half, keys_ref, values_ref, message_ref, pl.ds(0, half))
        total = first_ref[:, here].astype(F32) + second_ref[:, here].astype(F32)
        send_ref[...] = (total + message_ref[...].astype(F32)).astype(BF16)


def own_kernel(
    steps, place_ref, queries_ref, facts_ref, keys_ref, values_ref, first_ref, second_ref, keep_ref,
    message_ref,
):
    half = message_ref.shape[1]
    at = pl.multiple_of(lax.rem(place_ref[0], 2) * half, half)
    here = pl.ds(at, half)
    linked = is_linked(facts_ref, steps, place_ref[0])

    @pl.when(jnp.logical_not(linked))
    def _():
        keep_ref[...] = first_ref[:, here].astype(F32) + second_ref[:, here].astype(F32)

    @pl.when(linked)
    def _():
        attend(queries_ref, at, half, keys_ref, values_ref, message_ref, pl.ds(0, half))
        total = first_ref[:, here].astype(F32) + second_ref[:, here].astype(F32)
        keep_ref[...] = total + message_ref[...].astype(F32)


def tail_kernel(
    keep_ref, came_ref, rows_ref, out_ref, mlp_ref, vectors_ref, mlp_out_ref, result_ref
):
    width = keep_ref.shape[0]
    own_rows = rows_ref[...]
    hidden = dot(own_rows, mlp_ref[:width, :]) + vectors_ref[2:3, :]
    summed = (keep_ref[...] + came_ref[...].astype(F32)).astype(BF16)
    projected = dot(summed, out_ref[...], (0, 0)).astype(BF16)
    hidden = hidden + dot(projected, mlp_ref[width:, :])
    centered = hidden - jnp.mean(hidden, axis=1, keepdims=True)
    variance = jnp.mean(centered * centered, axis=1, keepdims=True)
    normed = centered * lax.rsqrt(variance + 1e-05) * vectors_ref[0:1, :] + vectors_ref[1:2, :]
    activated = (0.5 * normed * (1.0 + lax.erf(normed * math.sqrt(0.5)))).astype(BF16)
    updated = dot(activated, mlp_out_ref[...]) + vectors_ref[3:4, :width]
    result_ref[...] = (updated + own_rows.astype(F32)).astype(BF16)


def shape(dims, dtype):
    return jax.ShapeDtypeStruct(dims, dtype)


def cost(flops, moved, exps=0):
    return pl.CostEstimate(flops=flops, bytes_accessed=moved, transcendentals=exps)


def on_device(
    descriptors,
    links,
    qk_weight,
    value_weight,
    out_weight,
    mlp_in,
    mlp_in_bias,
    norm_gain,
    norm_bias,
    mlp_out,
    mlp_out_bias,
):
    own = descriptors[0]
    rows, width = own.shape
    hidden_width = mlp_in.shape[1]
    half = rows // 2
    images = lax.axis_size(("img", "pair"))
    place = lax.axis_index(RING).reshape(1)
    params = pltpu.CompilerParams(vmem_limit_bytes=40 << 20)

    own_weights = jnp.concatenate([qk_weight, value_weight], axis=1)
    swap = [(0, 1), (1, 0)]
    qk_other = lax.ppermute(qk_weight, "sub", swap)
    value_other = lax.ppermute(value_weight, "sub", swap)

    def carried(value, source):
        pairs = []
        for image in range(images):
            for sub in range(2):
                origin = source(image, sub)
                if origin is not None:
                    pairs.append((2 * origin[0] + origin[1], 2 * image + sub))
        return lax.ppermute(value, RING, pairs)

    def ahead(image, sub, step):
        partner = image + step if sub == 0 else image - step
        return partner if 0 <= partner < images else None

    def near(image, sub):
        return image % 2 == sub

    def within(image, sub):
        return (image ^ 1, image % 2) if near(image, sub) else None

    def by_two(image, sub):
        partner = ahead(image, sub, 2)
        return None if partner is None else (partner, sub)

    def outer(image, sub):
        partner = ahead(image, sub, 1)
        return None if near(image, sub) or partner is None else (partner, 1 - sub)

    def far_outer(image, sub):
        partner = ahead(image, sub, 3)
        if near(image, sub) or partner is None:
            return None
        return (partner ^ 1, (partner ^ 1) % 2)

    def far_inner(image, sub):
        if not near(image, sub) or ahead(image, sub, 3) is None:
            return None
        return (ahead(image, sub, 2), sub)

    one_inner = carried(own, within)
    two = carried(own, by_two)

    def called(kernel, args, out_shape, scratch, cost_estimate, scalars=1):
        return pl.pallas_call(
            kernel,
            in_specs=[SMEM] * scalars + [VMEM] * (len(args) - scalars),
            out_specs=[VMEM] * len(out_shape),
            out_shape=out_shape,
            scratch_shapes=scratch,
            compiler_params=params,
            cost_estimate=cost_estimate,
        )(*args)

    wk, wvt, queries, facts, own_half, vectors = called(
        functools.partial(prologue_kernel, images),
        [
            place, links.T, own, own_weights, qk_other, value_other,
            norm_gain.reshape(1, -1), norm_bias.reshape(1, -1), mlp_in_bias.reshape(1, -1),
            mlp_out_bias.reshape(1, -1),
        ],
        [
            shape((width, width), BF16),
            shape((width, width), BF16),
            shape((HEADS, 128, rows), BF16),
            shape((8, 128), F32),
            shape((half, width), BF16),
            shape((8, hidden_width), F32),
        ],
        [],
        cost(4 * rows * width * width, 4 << 20),
        scalars=2,
    )

    one_inner, facts, own_later = lax.optimization_barrier((one_inner, facts, own))
    three_outer = carried(one_inner, far_outer)
    three_inner = carried(one_inner, far_inner)
    one_outer = carried(own_later, outer)

    projected = [
        shape((rows, width), BF16),
        shape((HEADS, width // HEADS + 16, rows), BF16),
    ]
    scratch = [pltpu.VMEM(x.shape, x.dtype) for x in projected]
    message_shape = [shape((width, rows), BF16)]
    work = cost(8 * rows * rows * width, 2 << 20, HEADS * rows * rows)
    half_work = cost(4 * rows * rows * width, 2 << 20, HEADS * rows * half)
    (message,) = called(
        functools.partial(partner_kernel, (2, 2), False),
        [place, queries, facts, two, wk, wvt],
        message_shape,
        scratch,
        work,
    )
    three_outer, message = lax.optimization_barrier((three_outer, message))
    messages = [message]
    messages += called(
        functools.partial(partner_kernel, (1, 3), True),
        [place, queries, facts, three_outer, one_inner, wk, wvt],
        message_shape,
        scratch,
        work,
    )
    one_outer, three_inner, messages = lax.optimization_barrier((one_outer, three_inner, messages))
    keys, values, send = called(
        functools.partial(last_kernel, (3, 1)),
        [place, queries, facts, one_outer, three_inner, wk, wvt, *messages],
        [*projected, shape((width, half), BF16)],
        [pltpu.VMEM((width, half), BF16)],
        half_work,
    )
    came = lax.ppermute(send, "sub", swap)
    (keep,) = called(
        functools.partial(own_kernel, (3, 1)),
        [place, queries, facts, keys, values, *messages],
        [shape((width, half), F32)],
        [pltpu.VMEM((width, half), BF16)],
        half_work,
    )
    came, keep = lax.optimization_barrier((came, keep))
    (result,) = called(
        tail_kernel,
        [keep, came, own_half, out_weight, mlp_in, vectors, mlp_out],
        [shape((half, width), BF16)],
        [],
        cost(4 * rows * width * width, 4 << 20),
        scalars=0,
    )
    return result[None]


def solution(mesh):
    placed = (
        P(("groups", "img", "pair"), None, None),
        P("groups", None),
        P(None, "sub"),
        P(None, "sub"),
        P(),
        P(),
        P(),
        P(),
        P(),
        P(),
        P(),
    )

    return jax.shard_map(
        on_device,
        mesh=mesh,
        in_specs=placed,
        out_specs=P(("groups", "img", "pair"), "sub", None),
        check_vma=False,
    )
```

```python
import functools
import math

import jax
import jax.numpy as jnp
from jax import lax
from jax.experimental import pallas as pl
from jax.experimental.pallas import tpu as pltpu
from jax.sharding import PartitionSpec as P


HEADS = 4
SPAN = 3
RING = ("img", "pair", "sub")
LEAST_SUM, LARGEST_SUM = 1e-20, 1e20
LARGEST_PRODUCT = 1e37
F32 = jnp.float32
BF16 = jnp.bfloat16
VMEM = pl.BlockSpec(memory_space=pltpu.VMEM)
SMEM = pl.BlockSpec(memory_space=pltpu.SMEM)


def dot(a, b, contract=(1, 0)):
    return lax.dot_general(
        a, b, (((contract[0],), (contract[1],)), ((), ())), preferred_element_type=F32
    )


def prologue_kernel(
    images, place_ref, links_ref, x_ref, own_ref, qk_other_ref, value_other_ref, gain_ref,
    shift_ref, bias_ref, out_bias_ref, wk_ref, wvt_ref, queries_ref, facts_ref, rows_ref, vectors_ref,
):
    rows, width = x_ref.shape
    local = width // 2
    sub = lax.rem(place_ref[0], 2)
    image = place_ref[0] // 2
    parts = []
    for i, other_ref in enumerate((qk_other_ref, value_other_ref)):
        own, other = own_ref[:, i * local : (i + 1) * local], other_ref[...]
        parts.append(jnp.where(sub == 0, own, other))
        parts.append(jnp.where(sub == 0, other, own))
    wk_ref[:, :local], wk_ref[:, local:] = parts[0], parts[1]
    wvt_ref[:local, :], wvt_ref[local:, :] = parts[2].T, parts[3].T
    transposed = jnp.concatenate([parts[0].T, parts[1].T], axis=0)
    queries = dot(transposed, x_ref[...], (1, 1)).astype(BF16)
    head_width = width // HEADS
    for head in range(HEADS):
        mine, rest = (0, head_width) if head % 2 == 0 else (head_width, 0)
        queries_ref[head, mine : mine + head_width, :] = queries[
            head * head_width : (head + 1) * head_width, :
        ]
        queries_ref[head, rest : rest + head_width, :] = jnp.zeros((head_width, rows), BF16)
    for step in range(1, SPAN + 1):
        lower = image - sub * step
        inside = jnp.logical_and(lower >= 0, lower + step < images)
        entry = links_ref[step - 1, jnp.clip(lower, 0, images - 1)]
        linked = jnp.where(jnp.logical_and(inside, entry != 0), 1.0, 0.0)
        facts_ref[step : step + 1, :] = jnp.full((1, 128), linked, F32)
    half = rows // 2
    rows_ref[...] = x_ref[pl.ds(pl.multiple_of(sub * half, half), half), :]
    vectors_ref[0:1, :] = gain_ref[...]
    vectors_ref[1:2, :] = shift_ref[...]
    vectors_ref[2:3, :] = bias_ref[...]
    vectors_ref[3:4, :width] = out_bias_ref[...]


def project(x_ref, other_ref, take_other, wk_ref, wvt_ref, keys_ref, values_ref):
    rows, width = keys_ref.shape
    head_width = width // HEADS
    tile = 256
    for r in range(0, rows, tile):
        x = x_ref[r : r + tile, :]
        if other_ref is not None:
            x = jnp.where(take_other, other_ref[r : r + tile, :], x)
        keys_ref[r : r + tile, :] = dot(x, wk_ref[...]).astype(BF16)
        values = dot(wvt_ref[...], x, (1, 1)).astype(BF16)
        for head in range(HEADS):
            values_ref[head, :head_width, r : r + tile] = values[
                head * head_width : (head + 1) * head_width, :
            ]
            values_ref[head, head_width:, r : r + tile] = jnp.ones((16, tile), BF16)


def attend(queries_ref, at, span, keys_ref, values_ref, message_ref, into):
    rows, width = keys_ref.shape
    head_width = width // HEADS
    scale = 1.0 / math.sqrt(head_width)
    tile = 256
    queries_at = pl.ds(pl.multiple_of(at, span), span)
    totals = {}
    wrong = []

    def finish(head, r, scores):
        weights = jnp.exp2(scores * (scale * math.log2(math.e))).astype(BF16)
        product = dot(values_ref[head, :, r : r + tile], weights)
        total = product if r == 0 else totals[head] + product
        totals[head] = total
        if r + tile == rows:
            sums = total[head_width : head_width + 1]
            message_ref[head * head_width : (head + 1) * head_width, into] = (
                total[:head_width] * (1.0 / sums)
            ).astype(BF16)
            top = jnp.max(jnp.abs(total[:head_width]), axis=0, keepdims=True)
            fine = jnp.logical_and(sums > LEAST_SUM, sums < LARGEST_SUM)
            fine = jnp.logical_and(fine, top < LARGEST_PRODUCT)
            wrong.append(jnp.where(fine, 0.0, 1.0))

    waiting = []
    for head in range(HEADS):
        queries = queries_ref[head, :, queries_at]
        lanes = slice(head // 2 * 128, head // 2 * 128 + 128)
        for r in range(0, rows, tile):
            waiting.append((head, r, dot(keys_ref[r : r + tile, lanes], queries)))
            if len(waiting) > 2:
                finish(*waiting.pop(0))
    for item in waiting:
        finish(*item)

    @pl.when(jnp.max(sum(wrong)) > 0.0)
    def _():
        def body(i, carry):
            head, part = i // (span // tile), lax.rem(i, span // tile)
            part_at = pl.ds(pl.multiple_of(at + part * tile, tile), tile)
            lanes = pl.ds(pl.multiple_of(head // 2 * 128, 128), 128)
            scores = dot(keys_ref[:, lanes], queries_ref[head, :, part_at]) * scale
            powers = jnp.exp(scores - jnp.max(scores, axis=0, keepdims=True))
            weights = powers / jnp.sum(powers, axis=0, keepdims=True)
            product = dot(values_ref[head, :head_width, :], weights.astype(BF16))
            head_rows = pl.ds(pl.multiple_of(head * head_width, head_width), head_width)
            columns = pl.ds(pl.multiple_of(into.start + part * tile, tile), tile)
            message_ref[head_rows, columns] = product.astype(BF16)
            return carry

        lax.fori_loop(0, HEADS * (span // tile), body, 0)


def near_first(place):
    return lax.rem(place // 2, 2) == lax.rem(place, 2)


def partner_kernel(step, two, place_ref, queries_ref, facts_ref, x_ref, *refs):
    other_ref, *refs = refs if two else (None, *refs)
    wk_ref, wvt_ref, message_ref, keys_ref, values_ref = refs
    rows, _ = keys_ref.shape
    linked = jnp.max(facts_ref[step : step + 1, :]) > 0.0

    @pl.when(jnp.logical_not(linked))
    def _():
        message_ref[...] = jnp.zeros_like(message_ref)

    @pl.when(linked)
    def _():
        take = near_first(place_ref[0])
        project(x_ref, other_ref, take, wk_ref, wvt_ref, keys_ref, values_ref)
        wide = rows // 2

        def body(i, carry):
            at = pl.multiple_of(i * wide, wide)
            attend(queries_ref, at, wide, keys_ref, values_ref, message_ref, pl.ds(at, wide))
            return carry

        lax.fori_loop(0, rows // wide, body, 0)


def last_kernel(
    step, place_ref, queries_ref, facts_ref, x_ref, other_ref, wk_ref, wvt_ref, first_ref,
    second_ref, keys_ref, values_ref, send_ref, message_ref,
):
    half = message_ref.shape[1]
    place = place_ref[0]
    at = pl.multiple_of((1 - lax.rem(place, 2)) * half, half)
    here = pl.ds(at, half)
    linked = jnp.max(facts_ref[step : step + 1, :]) > 0.0
    total = first_ref[:, here].astype(F32) + second_ref[:, here].astype(F32)

    @pl.when(jnp.logical_not(linked))
    def _():
        send_ref[...] = total.astype(BF16)

    @pl.when(linked)
    def _():
        project(x_ref, other_ref, near_first(place), wk_ref, wvt_ref, keys_ref, values_ref)
        attend(queries_ref, at, half, keys_ref, values_ref, message_ref, pl.ds(0, half))
        total = first_ref[:, here].astype(F32) + second_ref[:, here].astype(F32)
        send_ref[...] = (total + message_ref[...].astype(F32)).astype(BF16)


def own_kernel(
    step, place_ref, queries_ref, facts_ref, keys_ref, values_ref, first_ref, second_ref, keep_ref,
    message_ref,
):
    half = message_ref.shape[1]
    at = pl.multiple_of(lax.rem(place_ref[0], 2) * half, half)
    here = pl.ds(at, half)
    linked = jnp.max(facts_ref[step : step + 1, :]) > 0.0

    @pl.when(jnp.logical_not(linked))
    def _():
        keep_ref[...] = first_ref[:, here].astype(F32) + second_ref[:, here].astype(F32)

    @pl.when(linked)
    def _():
        attend(queries_ref, at, half, keys_ref, values_ref, message_ref, pl.ds(0, half))
        total = first_ref[:, here].astype(F32) + second_ref[:, here].astype(F32)
        keep_ref[...] = total + message_ref[...].astype(F32)


def tail_kernel(
    keep_ref, came_ref, rows_ref, out_ref, mlp_ref, vectors_ref, mlp_out_ref, result_ref
):
    width = keep_ref.shape[0]
    own_rows = rows_ref[...]
    hidden = dot(own_rows, mlp_ref[:width, :]) + vectors_ref[2:3, :]
    summed = (keep_ref[...] + came_ref[...].astype(F32)).astype(BF16)
    projected = dot(summed, out_ref[...], (0, 0)).astype(BF16)
    hidden = hidden + dot(projected, mlp_ref[width:, :])
    centered = hidden - jnp.mean(hidden, axis=1, keepdims=True)
    variance = jnp.mean(centered * centered, axis=1, keepdims=True)
    normed = centered * lax.rsqrt(variance + 1e-05) * vectors_ref[0:1, :] + vectors_ref[1:2, :]
    activated = (0.5 * normed * (1.0 + lax.erf(normed * math.sqrt(0.5)))).astype(BF16)
    updated = dot(activated, mlp_out_ref[...]) + vectors_ref[3:4, :width]
    result_ref[...] = (updated + own_rows.astype(F32)).astype(BF16)


def shape(dims, dtype):
    return jax.ShapeDtypeStruct(dims, dtype)


def cost(flops, moved, exps=0):
    return pl.CostEstimate(flops=flops, bytes_accessed=moved, transcendentals=exps)


def on_device(
    descriptors,
    links,
    qk_weight,
    value_weight,
    out_weight,
    mlp_in,
    mlp_in_bias,
    norm_gain,
    norm_bias,
    mlp_out,
    mlp_out_bias,
):
    own = descriptors[0]
    rows, width = own.shape
    hidden_width = mlp_in.shape[1]
    half = rows // 2
    images = lax.axis_size(("img", "pair"))
    place = lax.axis_index(RING).reshape(1)
    params = pltpu.CompilerParams(vmem_limit_bytes=40 << 20)

    own_weights = jnp.concatenate([qk_weight, value_weight], axis=1)
    swap = [(0, 1), (1, 0)]
    qk_other = lax.ppermute(qk_weight, "sub", swap)
    value_other = lax.ppermute(value_weight, "sub", swap)

    def carried(value, source):
        pairs = []
        for image in range(images):
            for sub in range(2):
                origin = source(image, sub)
                if origin is not None:
                    pairs.append((2 * origin[0] + origin[1], 2 * image + sub))
        return lax.ppermute(value, RING, pairs)

    def ahead(image, sub, step):
        partner = image + step if sub == 0 else image - step
        return partner if 0 <= partner < images else None

    def near(image, sub):
        return image % 2 == sub

    def within(image, sub):
        return (image ^ 1, image % 2) if near(image, sub) else None

    def by_two(image, sub):
        partner = ahead(image, sub, 2)
        return None if partner is None else (partner, sub)

    def outer(image, sub):
        partner = ahead(image, sub, 1)
        return None if near(image, sub) or partner is None else (partner, 1 - sub)

    def far_outer(image, sub):
        partner = ahead(image, sub, 3)
        if near(image, sub) or partner is None:
            return None
        return (partner ^ 1, (partner ^ 1) % 2)

    def far_inner(image, sub):
        if not near(image, sub) or ahead(image, sub, 3) is None:
            return None
        return (ahead(image, sub, 2), sub)

    one_inner = carried(own, within)
    two = carried(own, by_two)

    def called(kernel, args, out_shape, scratch, cost_estimate, scalars=1):
        return pl.pallas_call(
            kernel,
            in_specs=[SMEM] * scalars + [VMEM] * (len(args) - scalars),
            out_specs=[VMEM] * len(out_shape),
            out_shape=out_shape,
            scratch_shapes=scratch,
            compiler_params=params,
            cost_estimate=cost_estimate,
        )(*args)

    wk, wvt, queries, facts, own_half, vectors = called(
        functools.partial(prologue_kernel, images),
        [
            place, links.T, own, own_weights, qk_other, value_other,
            norm_gain.reshape(1, -1), norm_bias.reshape(1, -1), mlp_in_bias.reshape(1, -1),
            mlp_out_bias.reshape(1, -1),
        ],
        [
            shape((width, width), BF16),
            shape((width, width), BF16),
            shape((HEADS, 128, rows), BF16),
            shape((8, 128), F32),
            shape((half, width), BF16),
            shape((8, hidden_width), F32),
        ],
        [],
        cost(4 * rows * width * width, 4 << 20),
        scalars=2,
    )

    own_later, facts = lax.optimization_barrier((own, facts))
    one_outer = carried(own_later, outer)
    one_inner, facts = lax.optimization_barrier((one_inner, facts))
    three_outer = carried(one_inner, far_outer)
    three_inner = carried(one_inner, far_inner)

    projected = [
        shape((rows, width), BF16),
        shape((HEADS, width // HEADS + 16, rows), BF16),
    ]
    scratch = [pltpu.VMEM(x.shape, x.dtype) for x in projected]
    message_shape = [shape((width, rows), BF16)]
    work = cost(8 * rows * rows * width, 2 << 20, HEADS * rows * rows)
    half_work = cost(4 * rows * rows * width, 2 << 20, HEADS * rows * half)
    (message,) = called(
        functools.partial(partner_kernel, 2, False),
        [place, queries, facts, two, wk, wvt],
        message_shape,
        scratch,
        work,
    )
    one_outer, message = lax.optimization_barrier((one_outer, message))
    messages = [message]
    messages += called(
        functools.partial(partner_kernel, 1, True),
        [place, queries, facts, one_outer, one_inner, wk, wvt],
        message_shape,
        scratch,
        work,
    )
    three_outer, three_inner, messages = lax.optimization_barrier(
        (three_outer, three_inner, messages)
    )
    keys, values, send = called(
        functools.partial(last_kernel, 3),
        [place, queries, facts, three_outer, three_inner, wk, wvt, *messages],
        [*projected, shape((width, half), BF16)],
        [pltpu.VMEM((width, half), BF16)],
        half_work,
    )
    came = lax.ppermute(send, "sub", swap)
    (keep,) = called(
        functools.partial(own_kernel, 3),
        [place, queries, facts, keys, values, *messages],
        [shape((width, half), F32)],
        [pltpu.VMEM((width, half), BF16)],
        half_work,
    )
    came, keep = lax.optimization_barrier((came, keep))
    (result,) = called(
        tail_kernel,
        [keep, came, own_half, out_weight, mlp_in, vectors, mlp_out],
        [shape((half, width), BF16)],
        [],
        cost(4 * rows * width * width, 4 << 20),
        scalars=0,
    )
    return result[None]


def solution(mesh):
    placed = (
        P(("groups", "img", "pair"), None, None),
        P("groups", None),
        P(None, "sub"),
        P(None, "sub"),
        P(),
        P(),
        P(),
        P(),
        P(),
        P(),
        P(),
    )

    return jax.shard_map(
        on_device,
        mesh=mesh,
        in_specs=placed,
        out_specs=P(("groups", "img", "pair"), "sub", None),
        check_vma=False,
    )
```
